128 devices in a mesh: sx: 16 (over z, y), sy: 8 (over x, core).
Axes of the slice: x: 4, y: 4, z: 4, core: 2. Of those that a mesh axis runs over, the one named last changes fastest.
Arguments:
- obs_values: bfloat16 [32768, 64], P(('sx', 'sy')), may hold values from -6 to 6
- obs_dest: int32 [32768, 1], P(('sx', 'sy')), may hold values from 0 to 127; in each aligned block of 256 rows (0 to 255, 256 to 511, ...) at most 4 rows name the same one
- obs_node: int32 [32768], P(('sx', 'sy')), may hold values from 0 to 2047
- schur: bfloat16 [16, 8, 2048, 2048], P('sx', 'sy'), as said below
- local_inverse: bfloat16 [16, 8, 2048, 2048], P('sx', 'sy'), as said below
- coarse_inverse: float32 [1024, 1024], P(('sx', 'sy')), as said below
Outputs:
- solution_field: float32 [16, 8, 64, 2048], P('sx', 'sy')
- residual: float32 [16, 8, 64, 2048], P('sx', 'sy')
The draws below stay inside these ranges and needn't reach their ends.
Inputs may be any that keep to these rules, and one draw needn't show every extreme that they name: `obs_dest`: at most 4 observations of one device go to one subdomain. `schur`: symmetric positive definite. `local_inverse`: symmetric positive definite. `coarse_inverse`: symmetric positive definite.
All inputs are finite; a program needn't handle non-finite values.
Results may differ from the reference program's by a relative error of at most 0.04.
Values may be sent and summed in bfloat16 or wider, within the bound.
A program may use at most 128 MiB of HBM per device.

```python
import math
import jax
import jax.numpy as jnp
import numpy as np
from jax import lax

SI = 2048
REAL = 64
NC = 8
ITERS = 6
OBS_DEV = 256
COLS = 16
ROWS = 8
CAP = 4
OBS_ALL = 32768
NCG = 1024
DEVICES = 128


def spd_matrix(key, lead, order, low, high, off_scale):
    first = jax.random.fold_in(key, 11)
    second = jax.random.fold_in(key, 23)
    base = jax.random.normal(first, lead + (order, order), jnp.float32)
    sym = (base + jnp.swapaxes(base, -1, -2)) * (off_scale / jnp.sqrt(2.0 * order))
    diag = jax.random.uniform(second, lead + (order,), jnp.float32, low, high)
    eye_mat = jnp.eye(order, dtype=jnp.float32)
    return sym + eye_mat * diag[..., :, None]


def draw_schur(key, part):
    return spd_matrix(key, (COLS, ROWS), SI, 1.0, 2.0, 0.3).astype(jnp.bfloat16)


def draw_local_inverse(key, part):
    return spd_matrix(key, (COLS, ROWS), SI, 0.5, 1.0, 0.15).astype(jnp.bfloat16)


def draw_coarse_inverse(key, part):
    return spd_matrix(key, (), NCG, 4.0, 8.0, 1.0)


def set_ends(result, stream_key, low, largest):
    longest = result.shape.index(max(result.shape))
    spots = []
    for shift in (0, 1):
        where = [jax.random.randint(jax.random.fold_in(stream_key, axis), (), 0, length) for axis, length in enumerate(result.shape)]
        where[longest] = (where[longest] + shift) % result.shape[longest]
        spots.append(tuple(where))
    return result.at[spots[0]].set(low).at[spots[1]].set(largest)


def steps_of(rng, shape, cuts, smallest, largest):
    level = 1.0
    for position, parts in cuts:
        heights = jax.random.uniform(jax.random.fold_in(jax.random.fold_in(rng, 6), position), (parts,), jnp.float32, smallest / len(cuts), largest / len(cuts))
        level = level * jnp.repeat(jnp.exp(heights), shape[position] // parts).reshape((-1,) + (1,) * (len(shape) - 1 - position))
    return level


def shared_out(own_key, own, number, rows, number_of, top, reach, slope):
    ranking = jax.random.permutation(own_key, number_of)
    crowded, usual = portions_of(number_of, rows * top, reach, slope, True), portions_of(number_of, rows * top, reach, slope, False)
    places = jnp.arange(number_of)

    def named(sizes, turn):
        used = int((sizes > 0).sum())
        fixed = max(1, used // 4)
        passed = fixed + (places - fixed + turn * (used - fixed)) % max(1, number_of - fixed)
        return jnp.zeros((number_of,), jnp.int32).at[ranking[jnp.where(places < fixed, places, passed)]].set(jnp.asarray(sizes, jnp.int32))

    sizes = jnp.where(number % 4 == 0, named(crowded, number // 4), named(usual, number - number // 4 - 1))
    mixed = jax.random.permutation(jax.random.fold_in(own, 3), number_of)
    donor, taker = mixed[0:number_of // 2 * 2:2], mixed[1:number_of // 2 * 2:2]
    room = jnp.minimum(sizes[donor] - 1, reach - sizes[taker]) // 2
    room = jnp.where((donor == ranking[0]) | (taker == ranking[0]) | (sizes[taker] == 0), 0, jnp.maximum(room, 0))
    passed = jax.random.randint(jax.random.fold_in(own, 4), (number_of // 2,), 0, 1 << 20) % (room + 1)
    sizes = sizes.at[donor].add(-passed).at[taker].add(passed)
    items = jnp.searchsorted(jnp.cumsum(sizes), jnp.arange(rows * top), side="right").astype(jnp.int32)
    grid = items.reshape(top, rows).T
    grid = grid[jax.random.permutation(jax.random.fold_in(own, 1), rows)]
    turn = jax.random.randint(jax.random.fold_in(own, 2), (rows, 1), 0, top)
    return jnp.take_along_axis(grid, (jnp.arange(top)[None, :] + turn) % top, axis=1)


def portions_of(count, total, limit, skew, full):
    weights = [(1 << 20) // math.isqrt(rank ** skew) + 1 for rank in range(1, count + 1)]
    largest = limit if full else min(limit, max(-(-total // count), total * weights[0] // sum(weights)))
    least = 1 if total - largest >= count - 1 else 0
    holding, rest = [largest] + [least] * (count - 1), total - largest - least * (count - 1)
    while rest > 0:
        candidates = [i for i in range(1, count) if holding[i] < largest] or [i for i in range(1, count) if holding[i] < limit]
        pool, budget = sum([weights[i] for i in candidates]), rest
        for i in candidates:
            extra = min(limit - holding[i], max(1, budget * weights[i] // pool), rest)
            holding[i] = holding[i] + extra
            rest = rest - extra
    return np.array(holding)


def normal_values(key, shape, deviation, bound, cuts=(), held_as=jnp.bfloat16):
    level = steps_of(key, shape, cuts, -0.22, 0.18) if cuts else 1.0
    array = jax.random.normal(key, shape, jnp.float32) * deviation * level
    return jnp.minimum(jnp.maximum(array, -bound), bound).astype(held_as)


def setup_inputs(seed: int = 0) -> dict:
    key_list = jax.random.split(jax.random.key(seed), 7)
    obs_values = normal_values(key_list[0], (OBS_ALL, REAL), 1.0, 6.0, ((0, 128),))
    obs_dest_keys = jax.random.split(jax.random.fold_in(key_list[1], 1), OBS_ALL // OBS_DEV)
    obs_dest_turns = jax.random.permutation(jax.random.fold_in(key_list[1], 3), OBS_ALL // OBS_DEV)
    obs_dest = jax.vmap(lambda own, number: shared_out(jax.random.fold_in(key_list[1], 2), own, number, OBS_DEV, DEVICES, 1, CAP, 2))(obs_dest_keys, obs_dest_turns).reshape((OBS_ALL, 1))
    obs_node = set_ends(jax.random.randint(key_list[2], (OBS_ALL,), 0, SI), jax.random.fold_in(key_list[2], 1), 0, SI - 1).astype(jnp.int32)
    schur = draw_schur(jax.random.fold_in(key_list[6], 71), 0)
    local_inverse = draw_local_inverse(jax.random.fold_in(key_list[6], 71), 0)
    coarse_inverse = draw_coarse_inverse(jax.random.fold_in(key_list[6], 71), 0)
    return {"obs_values": obs_values, "obs_dest": obs_dest, "obs_node": obs_node, "schur": schur, "local_inverse": local_inverse, "coarse_inverse": coarse_inverse}


def assemble(local):
    edge_len = SI // 4
    padded = jnp.pad(local, ((1, 1), (1, 1), (0, 0), (0, 0)))
    west = local[..., 0:edge_len] + padded[:-2, 1:-1, :, edge_len:2 * edge_len]
    east = local[..., edge_len:2 * edge_len] + padded[2:, 1:-1, :, 0:edge_len]
    south = local[..., 2 * edge_len:3 * edge_len] + padded[1:-1, :-2, :, 3 * edge_len:]
    north = local[..., 3 * edge_len:] + padded[1:-1, 2:, :, 2 * edge_len:3 * edge_len]
    return jnp.concatenate([west, east, south, north], axis=3)

def edge_weights():
    edge_len = SI // 4
    col = jnp.arange(COLS)[:, None, None, None]
    row = jnp.arange(ROWS)[None, :, None, None]
    side = (jnp.arange(SI) // edge_len)[None, None, None, :]
    shared = (side == 0) & (col > 0) | (side == 1) & (col < COLS - 1) | (side == 2) & (row > 0) | (side == 3) & (row < ROWS - 1)
    return jnp.where(shared, 0.5, 1.0).astype(jnp.float32)

def coarse_basis():
    edge_len = SI // 4
    node = jnp.arange(SI)
    side = node // edge_len
    offset = (node % edge_len).astype(jnp.float32) - (edge_len - 1) / 2.0
    norm_ramp = jnp.sqrt(jnp.float32(edge_len * (edge_len * edge_len - 1) / 12.0))
    column = jnp.arange(NC)
    on_edge = side[:, None] == (column // 2)[None, :]
    value = jnp.where((column % 2 == 0)[None, :], 1.0 / jnp.sqrt(jnp.float32(edge_len)), offset[:, None] / norm_ramp)
    return jnp.where(on_edge, value, 0.0).astype(jnp.float32)

def local_apply(mats, vec):
    flat_mats = mats.reshape(-1, SI, SI)
    flat_vec = vec.reshape(-1, REAL, SI).astype(jnp.bfloat16)
    out = lax.map(lambda pair: jnp.dot(pair[1], pair[0], preferred_element_type=jnp.float32), (flat_mats, flat_vec))
    return out.reshape(COLS, ROWS, REAL, SI)

def reference(obs_values, obs_dest, obs_node, schur, local_inverse, coarse_inverse):
    hp = lax.Precision.HIGHEST
    target = obs_dest[:, 0].astype(jnp.int32) * SI + obs_node.astype(jnp.int32)
    load = jax.ops.segment_sum(obs_values.astype(jnp.float32), target, num_segments=COLS * ROWS * SI)
    load = jnp.transpose(load.reshape(COLS, ROWS, SI, REAL), (0, 1, 3, 2))
    rhs = assemble(load)
    weight = edge_weights()
    basis = coarse_basis()

    def precond(vec):
        scaled = weight * vec
        part = local_apply(local_inverse, scaled)
        coarse = jnp.einsum('abrs,sk->abkr', scaled, basis, precision=hp).reshape(NCG, REAL)
        solved = jnp.dot(coarse_inverse, coarse, precision=hp).reshape(COLS, ROWS, NC, REAL)
        correction = jnp.einsum('abkr,sk->abrs', solved, basis, precision=hp)
        return assemble(weight * (part + correction))

    def inner(left, right):
        return lax.optimization_barrier(jnp.sum(weight * left * right, axis=(0, 1, 3)))
    solution_field = jnp.zeros_like(rhs)
    residual = rhs
    precon = precond(residual)
    direction = precon
    rz_now = inner(residual, precon)
    for step in range(ITERS):
        image = assemble(local_apply(schur, direction))
        alpha = rz_now / inner(direction, image)
        solution_field = solution_field + alpha[:, None] * direction
        residual = residual - alpha[:, None] * image
        if step < ITERS - 1:
            precon = precond(residual)
            rz_next = inner(residual, precon)
            direction = precon + (rz_next / rz_now)[:, None] * direction
            rz_now = rz_next
    return (solution_field, residual)
```

```python
import functools

import jax
import jax.numpy as jnp
from jax import lax
from jax.experimental import pallas as pl
from jax.experimental.pallas import tpu as pltpu
from jax.sharding import PartitionSpec as P

ITERS = 6
MESH = pl.DeviceIdType.MESH
F32 = jnp.float32
BF16 = jnp.bfloat16
HP = lax.Precision.HIGHEST
NT = (((1,), (1,)), ((), ()))


def split3(value):
    high = value.astype(BF16)
    rest = value - high.astype(F32)
    mid = rest.astype(BF16)
    low = (rest - mid.astype(F32)).astype(BF16)
    return jnp.concatenate([high, mid, low], axis=0)


def kernel(
    cols, rows,
    values_ref, dest_ref, node_ref, schur_hbm, inverse_hbm, coarse_ref,
    x_ref, r_ref,
    schur, inverse, obs_send, obs_mid, obs_got, k_send, k_got, k_stack,
    vec_b, d_ref, s_ref, z_ref, q_ref, sb_ref,
    lin_send, lin_got, sch_send, sch_got,
    pay1, got1, pay2, got2, state,
    mat_sem, obs_sem, k_sem, lin_sem, sch_sem, one_sem, two_sem, out_sem,
):
    a = lax.axis_index("sx")
    b = lax.axis_index("sy")
    size = schur.shape[0]
    edge = size // 4
    realiz = values_ref.shape[1]
    obs = values_ref.shape[0]
    count = coarse_ref.shape[1]
    per_col = 8 * rows

    def sx_peer(j):
        return (lax.rem(a + j, cols), b)

    def sy_peer(j):
        return (a, lax.rem(b + j, rows))

    barrier = pltpu.get_barrier_semaphore()
    for j in range(1, rows):
        pl.semaphore_signal(barrier, inc=1, device_id=sy_peer(j), device_id_type=MESH)
    for j in range(1, cols):
        pl.semaphore_signal(barrier, inc=1, device_id=sx_peer(j), device_id_type=MESH)

    load_inverse = pltpu.make_async_copy(inverse_hbm.at[0, 0], inverse, mat_sem.at[0])
    load_schur = pltpu.make_async_copy(schur_hbm.at[0, 0], schur, mat_sem.at[1])
    load_schur.start()
    load_inverse.start()

    nbr = (sx_peer(cols - 1), sx_peer(1), sy_peer(rows - 1), sy_peer(1))
    opposite = (1, 0, 3, 2)
    there = (a > 0, a < cols - 1, b > 0, b < rows - 1)
    mask = [jnp.where(t, 1.0, 0.0).astype(F32) for t in there]
    weight = [jnp.where(t, 0.5, 1.0).astype(F32) for t in there]
    span = [slice(e * edge, (e + 1) * edge) for e in range(4)]
    flat = 1.0 / float(edge) ** 0.5
    ramp_norm = (edge * (edge * edge - 1) / 12.0) ** 0.5
    ramp = (
        lax.broadcasted_iota(jnp.int32, (1, edge), 1).astype(F32) - (edge - 1) / 2.0
    ) * (1.0 / ramp_norm)

    target_col = dest_ref[...]
    target_row = jnp.transpose(
        jnp.broadcast_to(target_col.astype(F32), (obs, 128))
    )[0:1].astype(jnp.int32)
    first = lax.broadcasted_iota(jnp.int32, (obs, obs), 0)
    second = lax.broadcasted_iota(jnp.int32, (obs, obs), 1)
    earlier = jnp.where((target_col == target_row) & (first < second), 1.0, 0.0)
    slot_row = jnp.sum(earlier, axis=0, keepdims=True).astype(jnp.int32)
    place = (lax.rem(target_row, rows) * cols + target_row // rows) * 8 + slot_row
    node_col = jnp.transpose(
        jnp.broadcast_to(node_ref[...].astype(F32), (128, obs))
    ).astype(jnp.int32)
    lane = lax.broadcasted_iota(jnp.int32, (obs, 128), 1)
    wide = jnp.concatenate(
        [values_ref[...].astype(F32), jnp.zeros((obs, 128 - realiz), F32)], axis=1
    )
    row_data = jnp.where(
        lane == realiz,
        (node_col // 128).astype(F32),
        jnp.where(lane == realiz + 1, lax.rem(node_col, 128).astype(F32), wide),
    ).astype(BF16)
    for t in range(rows):
        part = cols * 8
        spot = lax.broadcasted_iota(jnp.int32, (part, obs), 0) + t * part
        pick = jnp.where(spot == place, 1.0, 0.0).astype(BF16)
        obs_send[t] = jnp.dot(pick, row_data, preferred_element_type=F32).reshape(
            cols, 8, 128
        )

    inv_rows = coarse_ref[...]
    index = lax.broadcasted_iota(jnp.int32, (8, count), 1)
    sub_col = index // per_col
    sub_row = lax.rem(index // 8, rows)
    side = lax.rem(index, 8) // 2
    shared = (
        ((side == 0) & (sub_col > 0))
        | ((side == 1) & (sub_col < cols - 1))
        | ((side == 2) & (sub_row > 0))
        | ((side == 3) & (sub_row < rows - 1))
    )
    from_west = pltpu.roll(inv_rows, per_col - 2, axis=1)
    from_east = pltpu.roll(inv_rows, count - (per_col - 2), axis=1)
    from_south = pltpu.roll(inv_rows, 6, axis=1)
    from_north = pltpu.roll(inv_rows, count - 6, axis=1)
    across = jnp.where(
        side == 0,
        from_west,
        jnp.where(side == 1, from_east, jnp.where(side == 2, from_south, from_north)),
    )
    combined = jnp.where(shared, 0.5 * (inv_rows + across), inv_rows)
    k_send[...] = jnp.zeros_like(k_send)
    for t in range(cols):
        k_send[t, :, 0:per_col] = combined[:, t * per_col : (t + 1) * per_col]

    state[...] = jnp.zeros_like(state)
    state[2] = jnp.ones_like(state[2])
    x_ref[...] = jnp.zeros_like(x_ref)
    d_ref[...] = jnp.zeros_like(d_ref)
    s_ref[...] = jnp.zeros_like(s_ref)

    pl.semaphore_wait(barrier, rows - 1 + cols - 1)

    for j in range(1, rows):
        pltpu.make_async_remote_copy(
            obs_send.at[lax.rem(b + j, rows)], obs_mid.at[j],
            obs_sem.at[0], obs_sem.at[1],
            device_id=sy_peer(j), device_id_type=MESH,
        ).start()
    for j in range(1, cols):
        pltpu.make_async_remote_copy(
            k_send.at[lax.rem(a + j, cols)], k_got.at[cols - j],
            k_sem.at[0], k_sem.at[1],
            device_id=sx_peer(j), device_id_type=MESH,
        ).start()
    obs_mid[0] = obs_send[b]
    k_got[0] = k_send[a]

    edge_of = lax.broadcasted_iota(jnp.int32, (8, size), 1) // edge
    offset = lax.rem(lax.broadcasted_iota(jnp.int32, (8, size), 1), edge).astype(F32)
    function = lax.broadcasted_iota(jnp.int32, (8, size), 0)
    basis = jnp.where(
        edge_of == function // 2,
        jnp.where(
            lax.rem(function, 2) == 0, flat, (offset - (edge - 1) / 2.0) * (1.0 / ramp_norm)
        ),
        0.0,
    ).astype(F32)
    basis3 = split3(basis)
    load_schur.wait()
    for e in range(4):
        made = jnp.dot(basis3, schur[:, span[e]], preferred_element_type=F32)
        sb_ref[:, span[e]] = split3(made[0:8] + made[8:16] + made[16:24])

    def wait_bytes(ref, sem):
        pltpu.make_async_copy(ref, ref, sem).wait()

    wait_bytes(obs_mid.at[pl.ds(1, rows - 1)], obs_sem.at[1])
    wait_bytes(obs_mid.at[pl.ds(1, rows - 1)], obs_sem.at[0])
    for j in range(1, cols):
        pltpu.make_async_remote_copy(
            obs_mid.at[:, lax.rem(a + j, cols)], obs_got.at[j],
            obs_sem.at[2], obs_sem.at[3],
            device_id=sx_peer(j), device_id_type=MESH,
        ).start()
    obs_got[0] = obs_mid[:, a]
    wait_bytes(k_got.at[pl.ds(1, cols - 1)], k_sem.at[1])
    wait_bytes(k_got.at[pl.ds(1, cols - 1)], k_sem.at[0])
    k_stack[...] = k_got[...].reshape(cols * 8, 128)
    wait_bytes(obs_got.at[pl.ds(1, cols - 1)], obs_sem.at[3])
    wait_bytes(obs_got.at[pl.ds(1, cols - 1)], obs_sem.at[2])

    got = obs_got[...].reshape(cols * rows * 8, 128)
    got_node = (got[:, realiz : realiz + 1] * 128.0 + got[:, realiz + 1 : realiz + 2])
    got_node = got_node.astype(jnp.int32)
    got_values = jnp.transpose(got)[0:realiz].astype(BF16)

    def sch_copy(e):
        return pltpu.make_async_remote_copy(
            sch_send.at[e], sch_got.at[opposite[e]],
            sch_sem.at[0, e], sch_sem.at[1, opposite[e]],
            device_id=nbr[e], device_id_type=MESH,
        )

    def lin_copy(e):
        return pltpu.make_async_remote_copy(
            lin_send.at[e], lin_got.at[opposite[e]],
            lin_sem.at[0, e], lin_sem.at[1, opposite[e]],
            device_id=nbr[e], device_id_type=MESH,
        )

    for e in range(4):
        at = lax.broadcasted_iota(jnp.int32, (cols * rows * 8, edge), 1) + e * edge
        hot = jnp.where(at == got_node, 1.0, 0.0).astype(BF16)
        q_ref[:, span[e]] = jnp.dot(got_values, hot, preferred_element_type=F32)
        sch_send[e] = q_ref[:, span[e]].astype(BF16)
        sch_copy(e).start()

    def global_round(parity):
        for j in range(1, rows):
            pltpu.make_async_remote_copy(
                pay1, got1.at[parity, b], out_sem.at[0], one_sem.at[parity],
                device_id=sy_peer(j), device_id_type=MESH,
            ).start()
        got1[parity, b] = pay1[...]
        wait_bytes(got1.at[parity, pl.ds(0, rows - 1)], one_sem.at[parity])
        wait_bytes(got1.at[parity, pl.ds(0, rows - 1)], out_sem.at[0])
        gathered = got1[parity]
        stack = gathered.reshape(rows * 8, 128)
        partial = jnp.dot(
            k_stack[:, 0:per_col], stack, precision=HP, preferred_element_type=F32
        )
        sums = jnp.sum(gathered, axis=0)
        left = lax.broadcasted_iota(jnp.int32, (8, 128), 1) < realiz
        for j in range(cols):
            pay2[j] = jnp.where(left, partial[j * 8 : (j + 1) * 8], sums)
        for j in range(1, cols):
            pltpu.make_async_remote_copy(
                pay2.at[j], got2.at[parity, j], out_sem.at[1], two_sem.at[parity],
                device_id=sx_peer(j), device_id_type=MESH,
            ).start()
        got2[parity, 0] = pay2[0]
        wait_bytes(got2.at[parity, pl.ds(1, cols - 1)], two_sem.at[parity])
        wait_bytes(got2.at[parity, pl.ds(1, cols - 1)], out_sem.at[1])
        return jnp.transpose(jnp.sum(got2[parity], axis=0))

    start_coarse = lax.dot_general(
        basis, q_ref[...], NT, precision=HP, preferred_element_type=F32
    )
    pay1[...] = jnp.concatenate([start_coarse, jnp.zeros((8, 128 - realiz), F32)], axis=1)
    total = global_round(1)
    state[0, :, 0:8] = total[0:realiz]
    for e in range(4):
        sch_copy(e).wait_send()
        sch_copy(opposite[e]).wait_recv()
        r_ref[:, span[e]] = q_ref[:, span[e]] + mask[e] * sch_got[e].astype(F32)
    load_inverse.wait()

    def step(k, carry):
        parity = lax.rem(k, 2)
        coarse = state[0]
        for e in range(4):
            vec_b[:, span[e]] = (weight[e] * r_ref[:, span[e]]).astype(BF16)
        sum_rq = jnp.zeros((realiz, 128), F32)
        for e in range(4):
            part = jnp.dot(vec_b[...], inverse[:, span[e]], preferred_element_type=F32)
            fix = coarse[:, 2 * e : 2 * e + 1] * flat + coarse[:, 2 * e + 1 : 2 * e + 2] * ramp
            local = weight[e] * (part + fix)
            lin_send[e] = local.astype(BF16)
            lin_copy(e).start()
            q_ref[:, span[e]] = local
            prod = local * r_ref[:, span[e]]
            for t in range(edge // 128):
                sum_rq += prod[:, t * 128 : (t + 1) * 128]
        sum_zs = jnp.zeros((realiz, 128), F32)
        for e in (2, 3, 0, 1):
            lin_copy(e).wait_send()
            lin_copy(opposite[e]).wait_recv()
            z = q_ref[:, span[e]] + mask[e] * lin_got[e].astype(F32)
            z_ref[:, span[e]] = z
            vec_b[:, span[e]] = z.astype(BF16)
            prod = (weight[e] * z) * s_ref[:, span[e]]
            for t in range(edge // 128):
                sum_zs += prod[:, t * 128 : (t + 1) * 128]
        sum_zy = jnp.zeros((realiz, 128), F32)
        for e in range(4):
            y = jnp.dot(vec_b[...], schur[:, span[e]], preferred_element_type=F32)
            sch_send[e] = y.astype(BF16)
            sch_copy(e).start()
            q_ref[:, span[e]] = y
            prod = z_ref[:, span[e]] * y
            for t in range(edge // 128):
                sum_zy += prod[:, t * 128 : (t + 1) * 128]
        made = lax.dot_general(sb_ref[...], vec_b[...], NT, preferred_element_type=F32)
        local_coarse = made[0:8] + made[8:16] + made[16:24]
        lane = lax.broadcasted_iota(jnp.int32, (realiz, 128), 1)
        dots = jnp.where(
            lane == 0,
            jnp.sum(sum_rq, axis=1, keepdims=True),
            jnp.where(
                lane == 1,
                jnp.sum(sum_zy, axis=1, keepdims=True),
                jnp.where(lane == 2, jnp.sum(sum_zs, axis=1, keepdims=True), 0.0),
            ),
        )
        pay1[...] = jnp.concatenate([local_coarse, jnp.transpose(dots)[0:8]], axis=1)
        total = global_round(parity)
        made_coarse = total[0:realiz]
        sums = total[realiz : 2 * realiz]
        rz = sums[:, 0:1]
        rz_old = state[2, :, 0:1]
        curv_old = state[3, :, 0:1]
        beta = rz / rz_old
        curv = sums[:, 1:2] + 2.0 * beta * sums[:, 2:3] + beta * beta * curv_old
        alpha = rz / curv
        state[2] = jnp.broadcast_to(rz, (realiz, 128))
        state[3] = jnp.broadcast_to(curv, (realiz, 128))
        image_coarse = made_coarse + beta * state[1, :, 0:8]
        state[1, :, 0:8] = image_coarse
        state[0, :, 0:8] = state[0, :, 0:8] - alpha * image_coarse
        for e in range(4):
            sch_copy(e).wait_send()
            sch_copy(opposite[e]).wait_recv()
            image = (
                q_ref[:, span[e]]
                + mask[e] * sch_got[e].astype(F32)
                + beta * s_ref[:, span[e]]
            )
            s_ref[:, span[e]] = image
            direction = z_ref[:, span[e]] + beta * d_ref[:, span[e]]
            d_ref[:, span[e]] = direction
            x_ref[:, span[e]] = x_ref[:, span[e]] + alpha * direction
            r_ref[:, span[e]] = r_ref[:, span[e]] - alpha * image
        return carry

    lax.fori_loop(0, ITERS, step, 0)


def body(cols, rows, obs_values, obs_dest, obs_node, schur, local_inverse, coarse_inverse):
    size = schur.shape[-1]
    edge = size // 4
    realiz = obs_values.shape[1]
    obs = obs_values.shape[0]
    vmem = pl.BlockSpec(memory_space=pltpu.VMEM)
    hbm = pl.BlockSpec(memory_space=pl.ANY)
    vector = pltpu.VMEM((realiz, size), F32)
    halo = pltpu.VMEM((4, realiz, edge), BF16)
    out = jax.ShapeDtypeStruct((realiz, size), F32)
    dma = pltpu.SemaphoreType.DMA
    found, residual = pl.pallas_call(
        functools.partial(kernel, cols, rows),
        out_shape=(out, out),
        in_specs=[vmem, vmem, vmem, hbm, hbm, vmem],
        out_specs=(vmem, vmem),
        scratch_shapes=[
            pltpu.VMEM((size, size), BF16),
            pltpu.VMEM((size, size), BF16),
            pltpu.VMEM((rows, cols, 8, 128), F32),
            pltpu.VMEM((rows, cols, 8, 128), F32),
            pltpu.VMEM((cols, rows, 8, 128), F32),
            pltpu.VMEM((cols, 8, 128), F32),
            pltpu.VMEM((cols, 8, 128), F32),
            pltpu.VMEM((cols * 8, 128), F32),
            pltpu.VMEM((realiz, size), BF16),
            vector, vector, vector, vector,
            pltpu.VMEM((24, size), BF16),
            halo, halo, halo, halo,
            pltpu.VMEM((8, 128), F32),
            pltpu.VMEM((2, rows, 8, 128), F32),
            pltpu.VMEM((cols, 8, 128), F32),
            pltpu.VMEM((2, cols, 8, 128), F32),
            pltpu.VMEM((4, realiz, 128), F32),
            dma((2,)), dma((4,)), dma((2,)), dma((2, 4)), dma((2, 4)),
            dma((2,)), dma((2,)), dma((2,)),
        ],
        compiler_params=pltpu.CompilerParams(
            collective_id=0, has_side_effects=True, vmem_limit_bytes=48 << 20
        ),
    )(obs_values, obs_dest, obs_node.reshape(1, obs), schur, local_inverse, coarse_inverse)
    return found[None, None], residual[None, None]


def solution(mesh):
    placed = (
        P(("sx", "sy"), None),
        P(("sx", "sy"), None),
        P(("sx", "sy")),
        P("sx", "sy", None, None),
        P("sx", "sy", None, None),
        P(("sx", "sy"), None),
    )
    return jax.shard_map(
        functools.partial(body, mesh.shape["sx"], mesh.shape["sy"]),
        mesh=mesh,
        in_specs=placed,
        out_specs=(P("sx", "sy", None, None), P("sx", "sy", None, None)),
        check_vma=False,
    )
```

```python
import functools

import jax
import jax.numpy as jnp
from jax import lax
from jax.experimental import pallas as pl
from jax.experimental.pallas import tpu as pltpu
from jax.sharding import PartitionSpec as P

ITERS = 6
MESH = pl.DeviceIdType.MESH
F32 = jnp.float32
BF16 = jnp.bfloat16
NT = (((1,), (1,)), ((), ()))


def split(value, parts):
    found = []
    for _ in range(parts):
        piece = value.astype(BF16)
        found.append(piece)
        value = value - piece.astype(F32)
    return found


def wait_bytes(ref, sem):
    pltpu.make_async_copy(ref, ref, sem).wait()


def kernel(
    cols, rows,
    values_hbm, dest_hbm, node_hbm, schur_hbm, inverse_hbm, coarse_hbm,
    x_ref, r_ref,
    values_ref, dest_ref, node_ref, coarse_ref, schur, inverse,
    obs_send, obs_mid, obs_got, k_send, k_got, k_row, k_side, k_cat,
    zb_ref, yb_ref, d_ref, s_ref, t_ref, z_ref, y_ref, h_ref, sb_ref,
    lin_send, lin_got, sch_send, sch_got,
    pay1, got1, pay2, got2, state, late_ref,
    in_sem, mat_sem, obs_sem, k_sem, side_sem, lin_sem, sch_sem, one_sem, two_sem, out_sem,
):
    a = lax.axis_index("sx")
    b = lax.axis_index("sy")
    size = schur.shape[0]
    edge = size // 4
    realiz = values_ref.shape[0]
    obs = values_ref.shape[1]
    count = coarse_ref.shape[1]
    per_col = 8 * rows
    chips = rows // 2

    def sx_peer(j):
        return (lax.rem(a + j, cols), b)

    def sy_peer(j):
        return (a, lax.rem(b + j, rows))

    small = [
        pltpu.make_async_copy(dest_hbm, dest_ref, in_sem.at[0]),
        pltpu.make_async_copy(node_hbm, node_ref, in_sem.at[1]),
        pltpu.make_async_copy(values_hbm, values_ref, in_sem.at[2]),
        pltpu.make_async_copy(coarse_hbm, coarse_ref, in_sem.at[3]),
    ]
    for copy in small:
        copy.start()
    barrier = pltpu.get_barrier_semaphore()
    for j in range(1, cols):
        pl.semaphore_signal(barrier, inc=1, device_id=sx_peer(j), device_id_type=MESH)
    for j in range(1, rows):
        pl.semaphore_signal(barrier, inc=1, device_id=sy_peer(j), device_id_type=MESH)
    load_schur = pltpu.make_async_copy(schur_hbm.at[0, 0], schur, mat_sem.at[1])
    load_inverse = pltpu.make_async_copy(inverse_hbm.at[0, 0], inverse, mat_sem.at[0])
    load_schur.start()
    load_inverse.start()

    nbr = (sx_peer(cols - 1), sx_peer(1), sy_peer(rows - 1), sy_peer(1))
    opposite = (1, 0, 3, 2)
    there = (a > 0, a < cols - 1, b > 0, b < rows - 1)
    mask = [jnp.where(t, 1.0, 0.0).astype(F32) for t in there]
    weight = [jnp.where(t, 0.5, 1.0).astype(F32) for t in there]
    span = [slice(e * edge, (e + 1) * edge) for e in range(4)]
    flat = 1.0 / float(edge) ** 0.5
    ramp_norm = (edge * (edge * edge - 1) / 12.0) ** 0.5
    ramp = (
        lax.broadcasted_iota(jnp.int32, (1, edge), 1).astype(F32) - (edge - 1) / 2.0
    ) * (1.0 / ramp_norm)

    small[0].wait()
    target_row = dest_ref[...]
    target_col = jnp.transpose(
        jnp.broadcast_to(target_row.astype(F32), (128, obs))
    )[:, 0:1].astype(jnp.int32)
    first = lax.broadcasted_iota(jnp.int32, (obs, obs), 0)
    second = lax.broadcasted_iota(jnp.int32, (obs, obs), 1)
    earlier = jnp.where((target_col == target_row) & (first < second), 1.0, 0.0)
    slot_row = jnp.sum(earlier, axis=0, keepdims=True).astype(jnp.int32)
    place = target_row * 4 + slot_row
    small[1].wait()
    small[2].wait()
    node = node_ref[...]
    below = lax.broadcasted_iota(jnp.int32, (128 - realiz, obs), 0)
    tail = jnp.where(
        below == 0,
        (node // 128).astype(F32),
        jnp.where(below == 1, lax.rem(node, 128).astype(F32), 0.0),
    )
    row_data = jnp.concatenate([values_ref[...], tail.astype(BF16)], axis=0)
    for t in range(4):
        part = cols * rows
        spot = lax.broadcasted_iota(jnp.int32, (part, obs), 0) + t * part
        pick = jnp.where(spot == place, 1.0, 0.0).astype(BF16)
        made = lax.dot_general(pick, row_data, NT, preferred_element_type=F32)
        obs_send[t * cols // 4 : (t + 1) * cols // 4] = made.reshape(
            cols // 4, chips, 8, 128
        ).astype(BF16)

    pl.semaphore_wait(barrier, rows - 1 + cols - 1)

    for j in range(1, cols):
        pltpu.make_async_remote_copy(
            obs_send.at[lax.rem(a + j, cols)], obs_mid.at[j],
            obs_sem.at[0], obs_sem.at[1],
            device_id=sx_peer(j), device_id_type=MESH,
        ).start()
    obs_mid[0] = obs_send[a]

    small[3].wait()
    inv_rows = coarse_ref[...]
    index = lax.broadcasted_iota(jnp.int32, (8, count), 1)
    sub_col = index // per_col
    sub_row = lax.rem(index // 8, rows)
    side = lax.rem(index, 8) // 2
    shared = (
        ((side == 0) & (sub_col > 0))
        | ((side == 1) & (sub_col < cols - 1))
        | ((side == 2) & (sub_row > 0))
        | ((side == 3) & (sub_row < rows - 1))
    )
    from_west = pltpu.roll(inv_rows, per_col - 2, axis=1)
    from_east = pltpu.roll(inv_rows, count - (per_col - 2), axis=1)
    from_south = pltpu.roll(inv_rows, 6, axis=1)
    from_north = pltpu.roll(inv_rows, count - 6, axis=1)
    across = jnp.where(
        side == 0,
        from_west,
        jnp.where(side == 1, from_east, jnp.where(side == 2, from_south, from_north)),
    )
    combined = jnp.where(shared, 0.5 * (inv_rows + across), inv_rows)
    k_send[...] = jnp.zeros_like(k_send)
    for t in range(cols):
        k_send[t, :, 0:per_col] = combined[:, t * per_col : (t + 1) * per_col]
    for j in range(1, cols):
        pltpu.make_async_remote_copy(
            k_send.at[lax.rem(a + j, cols)], k_got.at[cols - j],
            k_sem.at[0], k_sem.at[1],
            device_id=sx_peer(j), device_id_type=MESH,
        ).start()
    k_got[0] = k_send[a]

    wait_bytes(obs_mid.at[pl.ds(1, cols - 1)], obs_sem.at[1])
    for j in range(1, rows):
        pltpu.make_async_remote_copy(
            obs_mid.at[:, lax.rem(b + j, rows) // 2], obs_got.at[j],
            obs_sem.at[2], obs_sem.at[3],
            device_id=sy_peer(j), device_id_type=MESH,
        ).start()
    obs_got[0] = obs_mid[:, b // 2]

    wait_bytes(k_got.at[pl.ds(1, cols - 1)], k_sem.at[1])
    k_row[...] = k_got[...].reshape(cols * 8, 128)
    side_copy = [
        pltpu.make_async_remote_copy(
            k_row, k_side.at[i], side_sem.at[0, i], side_sem.at[1, i],
            device_id=sy_peer(step), device_id_type=MESH,
        )
        for i, step in ((0, 1), (1, rows - 1))
    ]
    for copy in side_copy:
        copy.start()

    edge_of = lax.broadcasted_iota(jnp.int32, (8, size), 1) // edge
    offset = lax.rem(lax.broadcasted_iota(jnp.int32, (8, size), 1), edge).astype(F32)
    function = lax.broadcasted_iota(jnp.int32, (8, size), 0)
    basis = jnp.where(
        edge_of == function // 2,
        jnp.where(
            lax.rem(function, 2) == 0, flat, (offset - (edge - 1) / 2.0) * (1.0 / ramp_norm)
        ),
        0.0,
    ).astype(F32)
    basis3 = jnp.concatenate(split(basis, 3), axis=0)
    load_schur.wait()
    for e in range(4):
        made = jnp.dot(basis3, schur[:, span[e]], preferred_element_type=F32)
        sb_ref[:, span[e]] = jnp.concatenate(
            split(made[0:8] + made[8:16] + made[16:24], 2), axis=0
        )
    state[0] = jnp.ones_like(state[0])
    state[1] = jnp.zeros_like(state[1])
    x_ref[...] = jnp.zeros_like(x_ref)
    d_ref[...] = jnp.zeros_like(d_ref)
    s_ref[...] = jnp.zeros_like(s_ref)
    t_ref[...] = jnp.zeros_like(t_ref)
    pay1[...] = jnp.zeros_like(pay1)

    wait_bytes(obs_got.at[pl.ds(1, rows - 1)], obs_sem.at[3])
    got = obs_got[...].astype(F32).reshape(cols * rows * 8, 128)
    own_half = lax.rem(lax.broadcasted_iota(jnp.int32, (cols * rows * 8, 1), 0), 8) // 4
    got_node = got[:, realiz : realiz + 1] * 128.0 + got[:, realiz + 1 : realiz + 2]
    got_node = jnp.where(own_half == lax.rem(b, 2), got_node.astype(jnp.int32), -1)
    got_values = jnp.transpose(got)[0:realiz].astype(BF16)

    def sch_copy(i, parity=0):
        e, part = i % 4, i // 4
        at = opposite[e] + 4 * part * (1 + parity)
        return pltpu.make_async_remote_copy(
            sch_send.at[i], sch_got.at[at], sch_sem.at[0, i], sch_sem.at[1, at],
            device_id=nbr[e], device_id_type=MESH,
        )

    def lin_copy(i, parity=0):
        e, part = i % 4, i // 4
        at = opposite[e] + 4 * part * (1 + parity)
        return pltpu.make_async_remote_copy(
            lin_send.at[i], lin_got.at[at], lin_sem.at[0, i], lin_sem.at[1, at],
            device_id=nbr[e], device_id_type=MESH,
        )

    def send_partial(e, y):
        y_ref[:, span[e]] = y
        high, low = split(y, 2)
        sch_send[e] = high
        sch_copy(e).start()
        sch_send[4 + e] = low

    def send_payload(parity):
        for j in range(1, rows):
            pltpu.make_async_remote_copy(
                pay1, got1.at[parity, b], out_sem.at[0], one_sem.at[parity],
                device_id=sy_peer(j), device_id_type=MESH,
            ).start()
        got1[parity, b] = pay1[...]
        for e in range(4):
            sch_copy(4 + e, parity).start()

    def pass_payload(parity):
        wait_bytes(got1.at[parity, pl.ds(0, rows - 1)], one_sem.at[parity])
        wait_bytes(got1.at[parity, pl.ds(0, rows - 1)], out_sem.at[0])
        gathered = got1[parity]
        high, low = split(gathered.reshape(rows * 8, 128), 2)
        stack = jnp.concatenate([high, low, high], axis=0)
        partial = jnp.dot(k_cat[...], stack, preferred_element_type=F32)
        sums = jnp.sum(gathered, axis=0)
        left = lax.broadcasted_iota(jnp.int32, (8, 128), 1) < realiz
        for j in range(1, cols):
            pay2[j] = jnp.where(left, partial[j * 8 : (j + 1) * 8], sums)
            pltpu.make_async_remote_copy(
                pay2.at[j], got2.at[parity, j], out_sem.at[1], two_sem.at[parity],
                device_id=sx_peer(j), device_id_type=MESH,
            ).start()
        got2[parity, 0] = jnp.where(left, partial[0:8], sums)

    def take_payload(parity):
        wait_bytes(got2.at[parity, pl.ds(1, cols - 1)], two_sem.at[parity])
        wait_bytes(got2.at[parity, pl.ds(1, cols - 1)], out_sem.at[1])
        return jnp.transpose(jnp.sum(got2[parity], axis=0))

    def finish_image(e, parity):
        sch_copy(4 + e, parity).wait_send()
        sch_copy(4 + opposite[e], parity).wait_recv()
        return y_ref[:, span[e]] + mask[e] * sch_got[4 + 4 * parity + e].astype(F32)

    def take_high(e):
        sch_copy(e).wait_send()
        sch_copy(opposite[e]).wait_recv()
        y_ref[:, span[e]] = y_ref[:, span[e]] + mask[e] * sch_got[e].astype(F32)

    def put_y(e):
        high, low = split(weight[e] * y_ref[:, span[e]], 2)
        yb_ref[0:realiz, span[e]] = high
        yb_ref[realiz:, span[e]] = low

    def apply_inverse(parity):
        for e in (2, 3):
            take_high(e)
            y_ref[:, span[e]] = finish_image(e, parity)
            put_y(e)
        pass_payload(parity)
        for e in (0, 1):
            take_high(e)
            put_y(e)
        for e in range(4):
            made = jnp.dot(yb_ref[...], inverse[:, span[e]], preferred_element_type=F32)
            local = weight[e] * (made[0:realiz] + made[realiz:])
            high, low = split(local, 2)
            lin_send[e] = high
            lin_copy(e).start()
            lin_send[4 + e] = low
            h_ref[:, span[e]] = local
        for e in range(4):
            lin_copy(4 + e, parity).start()

    def coarse_part(e, total):
        return (
            total[0:realiz, 2 * e : 2 * e + 1] * flat
            + total[0:realiz, 2 * e + 1 : 2 * e + 2] * ramp
        )

    def take_lin(e):
        lin_copy(e).wait_send()
        lin_copy(opposite[e]).wait_recv()
        return mask[e] * lin_got[e].astype(F32)

    def take_low(e, alpha, once, parity):
        lin_copy(4 + e, parity).wait_send()
        lin_copy(4 + opposite[e], parity).wait_recv()
        low = mask[e] * lin_got[4 + 4 * parity + e].astype(F32)
        t_ref[:, span[e]] = t_ref[:, span[e]] + once * low
        late_ref[:, span[e]] = alpha * low

    def put_z(e, z):
        z_ref[:, span[e]] = z
        high, low = split(z, 2)
        zb_ref[0:realiz, span[e]] = high
        zb_ref[realiz:, span[e]] = low

    for e in range(4):
        at = lax.broadcasted_iota(jnp.int32, (cols * rows * 8, edge), 1) + e * edge
        hot = jnp.where(at == got_node, 1.0, 0.0).astype(BF16)
        send_partial(e, jnp.dot(got_values, hot, preferred_element_type=F32))
    loads = jnp.concatenate(split(y_ref[...], 2), axis=0)
    made = lax.dot_general(basis3, loads, NT, preferred_element_type=F32)
    made = made[0:8] + made[8:16] + made[16:24]
    pay1[:, 0:realiz] = made[:, 0:realiz] + made[:, realiz:]
    send_payload(1)

    for copy in side_copy:
        copy.wait_recv()
    rows_here = k_row[...]
    line = lax.broadcasted_iota(jnp.int32, (cols * 8, 1), 0)
    where_to = lax.rem(line // 8 + a, cols)
    line_side = lax.rem(line, 8) // 2
    k_west = jnp.where(where_to > 0, pltpu.roll(rows_here, 6, axis=0), 0.0)
    k_east = jnp.where(
        where_to < cols - 1, pltpu.roll(rows_here, cols * 8 - 6, axis=0), 0.0
    )
    k_south = mask[2] * pltpu.roll(k_side[0], cols * 8 - 2, axis=0)
    k_north = mask[3] * pltpu.roll(k_side[1], 2, axis=0)
    scale = jnp.where(
        line_side == 0,
        jnp.where(where_to > 0, 0.5, 1.0),
        jnp.where(
            line_side == 1,
            jnp.where(where_to < cols - 1, 0.5, 1.0),
            jnp.where(line_side == 2, weight[2], weight[3]),
        ),
    )
    rows_across = jnp.where(
        line_side == 0,
        k_west,
        jnp.where(line_side == 1, k_east, jnp.where(line_side == 2, k_south, k_north)),
    )
    k_high, k_low = split((scale * (rows_here + rows_across))[:, 0:per_col], 2)
    k_cat[...] = jnp.concatenate([k_high, k_high, k_low], axis=1)
    load_inverse.wait()

    apply_inverse(1)
    for e in (0, 1):
        r_ref[:, span[e]] = finish_image(e, 1)
    for e in (2, 3):
        r_ref[:, span[e]] = y_ref[:, span[e]]
    total = take_payload(1)
    for e in (2, 3, 0, 1):
        put_z(e, h_ref[:, span[e]] + coarse_part(e, total) + take_lin(e))
    state[2] = -jnp.ones_like(state[2])

    def apply_schur(parity):
        sum_rz = jnp.zeros((realiz, 128), F32)
        sum_zy = jnp.zeros((realiz, 128), F32)
        sum_zs = jnp.zeros((realiz, 128), F32)
        for e in range(4):
            made = jnp.dot(zb_ref[...], schur[:, span[e]], preferred_element_type=F32)
            y = made[0:realiz] + made[realiz:]
            send_partial(e, y)
            z = z_ref[:, span[e]]
            zw = weight[e] * z
            zy, zs, rz = z * y, zw * s_ref[:, span[e]], zw * r_ref[:, span[e]]
            for t in range(edge // 128):
                tile = slice(t * 128, (t + 1) * 128)
                sum_rz += rz[:, tile]
                sum_zy += zy[:, tile]
                sum_zs += zs[:, tile]
        made = lax.dot_general(sb_ref[...], zb_ref[...], NT, preferred_element_type=F32)
        made = made[0:8] + made[8:16]
        pay1[:, 0:realiz] = made[:, 0:realiz] + made[:, realiz:]
        lane = lax.broadcasted_iota(jnp.int32, (realiz, 128), 1)
        dots = jnp.where(
            lane == 0,
            jnp.sum(sum_rz, axis=1, keepdims=True),
            jnp.where(
                lane == 1,
                jnp.sum(sum_zy, axis=1, keepdims=True),
                jnp.where(lane == 2, jnp.sum(sum_zs, axis=1, keepdims=True), 0.0),
            ),
        )
        pay1[:, realiz:] = jnp.transpose(dots)[0:8]
        send_payload(parity)

    def factors(total):
        sums = total[realiz : 2 * realiz]
        rz = sums[:, 0:1]
        beta = rz / state[0, :, 0:1]
        curv = sums[:, 1:2] + beta * (2.0 * sums[:, 2:3] + beta * state[1, :, 0:1])
        state[0] = jnp.broadcast_to(rz, (realiz, 128))
        state[1] = jnp.broadcast_to(curv, (realiz, 128))
        state[2] = jnp.broadcast_to(rz / curv, (realiz, 128))
        return rz / curv, beta

    def advance(e, alpha, beta):
        image = y_ref[:, span[e]] + beta * s_ref[:, span[e]]
        s_ref[:, span[e]] = image
        direction = z_ref[:, span[e]] + beta * d_ref[:, span[e]]
        d_ref[:, span[e]] = direction
        x_ref[:, span[e]] = x_ref[:, span[e]] + alpha * direction
        r_ref[:, span[e]] = r_ref[:, span[e]] - alpha * image

    def step(k, carry):
        parity = lax.rem(k, 2)
        apply_schur(parity)
        for e in range(4):
            take_low(e, state[2, :, 0:1], jnp.where(k > 0, 1.0, 0.0).astype(F32), 1 - parity)
        apply_inverse(parity)
        for e in (0, 1):
            y_ref[:, span[e]] = finish_image(e, parity)
        total = take_payload(parity)
        alpha, beta = factors(total)
        for e in range(4):
            advance(e, alpha, beta)
            z_ref[:, span[e]] = z_ref[:, span[e]] - late_ref[:, span[e]]
            moved = h_ref[:, span[e]] + coarse_part(e, total) + beta * t_ref[:, span[e]]
            t_ref[:, span[e]] = moved
            z_ref[:, span[e]] = z_ref[:, span[e]] - alpha * moved
        for e in (2, 3, 0, 1):
            came = take_lin(e)
            t_ref[:, span[e]] = t_ref[:, span[e]] + came
            put_z(e, z_ref[:, span[e]] - alpha * came)
        return carry

    lax.fori_loop(0, ITERS - 1, step, 0)
    last = (ITERS - 1) % 2
    apply_schur(last)
    for e in range(4):
        lin_copy(4 + e, 1 - last).wait_send()
        lin_copy(4 + opposite[e], 1 - last).wait_recv()
    pass_payload(last)
    for e in range(4):
        take_high(e)
        y_ref[:, span[e]] = finish_image(e, last)
    alpha, beta = factors(take_payload(last))
    for e in range(4):
        advance(e, alpha, beta)

    wait_bytes(obs_mid.at[pl.ds(1, cols - 1)], obs_sem.at[0])
    wait_bytes(obs_got.at[pl.ds(1, rows - 1)], obs_sem.at[2])
    wait_bytes(k_got.at[pl.ds(1, cols - 1)], k_sem.at[0])
    for copy in side_copy:
        copy.wait_send()


def body(cols, rows, obs_values, obs_dest, obs_node, schur, local_inverse, coarse_inverse):
    size = schur.shape[-1]
    edge = size // 4
    realiz = obs_values.shape[1]
    obs = obs_values.shape[0]
    count = coarse_inverse.shape[1]
    vmem = pl.BlockSpec(memory_space=pltpu.VMEM)
    hbm = pl.BlockSpec(memory_space=pltpu.HBM)
    vector = pltpu.VMEM((realiz, size), F32)
    halved = pltpu.VMEM((2 * realiz, size), BF16)
    out = jax.ShapeDtypeStruct((realiz, size), F32)
    dma = pltpu.SemaphoreType.DMA
    found, residual = pl.pallas_call(
        functools.partial(kernel, cols, rows),
        out_shape=(out, out),
        in_specs=[hbm] * 6,
        out_specs=(vmem, vmem),
        scratch_shapes=[
            pltpu.VMEM((realiz, obs), BF16),
            pltpu.VMEM((1, obs), jnp.int32),
            pltpu.VMEM((1, obs), jnp.int32),
            pltpu.VMEM((8, count), F32),
            pltpu.VMEM((size, size), BF16),
            pltpu.VMEM((size, size), BF16),
            pltpu.VMEM((cols, rows // 2, 8, 128), BF16),
            pltpu.VMEM((cols, rows // 2, 8, 128), BF16),
            pltpu.VMEM((rows, cols, 8, 128), BF16),
            pltpu.VMEM((cols, 8, 128), F32),
            pltpu.VMEM((cols, 8, 128), F32),
            pltpu.VMEM((cols * 8, 128), F32),
            pltpu.VMEM((2, cols * 8, 128), F32),
            pltpu.VMEM((cols * 8, 3 * 8 * rows), BF16),
            halved, halved,
            vector, vector, vector, vector, vector, vector,
            pltpu.VMEM((16, size), BF16),
            pltpu.VMEM((8, realiz, edge), BF16),
            pltpu.VMEM((12, realiz, edge), BF16),
            pltpu.VMEM((8, realiz, edge), BF16),
            pltpu.VMEM((12, realiz, edge), BF16),
            pltpu.VMEM((8, 128), F32),
            pltpu.VMEM((2, rows, 8, 128), F32),
            pltpu.VMEM((cols, 8, 128), F32),
            pltpu.VMEM((2, cols, 8, 128), F32),
            pltpu.VMEM((3, realiz, 128), F32), vector,
            dma((4,)), dma((2,)), dma((4,)), dma((2,)), dma((2, 2)),
            dma((2, 12)), dma((2, 12)), dma((2,)), dma((2,)), dma((2,)),
        ],
        compiler_params=pltpu.CompilerParams(
            collective_id=0, has_side_effects=True, vmem_limit_bytes=48 << 20
        ),
    )(
        obs_values.T, obs_dest.reshape(1, obs), obs_node.reshape(1, obs),
        schur, local_inverse, coarse_inverse,
    )
    return found[None, None], residual[None, None]


def solution(mesh):
    placed = (
        P(("sx", "sy"), None),
        P(("sx", "sy"), None),
        P(("sx", "sy")),
        P("sx", "sy", None, None),
        P("sx", "sy", None, None),
        P(("sx", "sy"), None),
    )
    return jax.shard_map(
        functools.partial(body, mesh.shape["sx"], mesh.shape["sy"]),
        mesh=mesh,
        in_specs=placed,
        out_specs=(P("sx", "sy", None, None), P("sx", "sy", None, None)),
        check_vma=False,
    )
```

```python
import functools

import jax
import jax.numpy as jnp
from jax import lax
from jax.experimental import pallas as pl
from jax.experimental.pallas import tpu as pltpu
from jax.sharding import PartitionSpec as P

ITERS = 6
MESH = pl.DeviceIdType.MESH
F32 = jnp.float32
BF16 = jnp.bfloat16
NT = (((1,), (1,)), ((), ()))


def split(value, parts):
    found = []
    for _ in range(parts):
        piece = value.astype(BF16)
        found.append(piece)
        value = value - piece.astype(F32)
    return found


def wait_bytes(ref, sem):
    pltpu.make_async_copy(ref, ref, sem).wait()


def kernel(
    cols, rows,
    values_hbm, dest_hbm, node_hbm, schur_hbm, inverse_hbm, coarse_hbm,
    x_ref, r_ref,
    values_ref, dest_ref, node_ref, coarse_ref, schur, inverse,
    obs_send, obs_mid, obs_got, k_send, k_got, k_row, k_side, k_cat,
    zb_ref, yb_ref, d_ref, s_ref, t_ref, z_ref, y_ref, h_ref, acc_ref, acc_g, sb_ref,
    lin_send, lin_got, sch_send, sch_got,
    pay1, got1, pay2, got2, state, late_ref,
    in_sem, mat_sem, obs_sem, k_sem, side_sem, lin_sem, sch_sem, one_sem, two_sem, out_sem,
):
    a = lax.axis_index("sx")
    b = lax.axis_index("sy")
    size = schur.shape[0]
    edge = size // 4
    realiz = values_ref.shape[0]
    obs = values_ref.shape[1]
    count = coarse_ref.shape[1]
    per_col = 8 * rows
    chips = rows // 2

    def sx_peer(j):
        return (lax.rem(a + j, cols), b)

    def sy_peer(j):
        return (a, lax.rem(b + j, rows))

    small = [
        pltpu.make_async_copy(dest_hbm, dest_ref, in_sem.at[0]),
        pltpu.make_async_copy(node_hbm, node_ref, in_sem.at[1]),
        pltpu.make_async_copy(values_hbm, values_ref, in_sem.at[2]),
        pltpu.make_async_copy(coarse_hbm, coarse_ref, in_sem.at[3]),
    ]
    for copy in small:
        copy.start()
    barrier = pltpu.get_barrier_semaphore()
    for j in range(1, cols):
        pl.semaphore_signal(barrier, inc=1, device_id=sx_peer(j), device_id_type=MESH)
    for j in range(1, rows):
        pl.semaphore_signal(barrier, inc=1, device_id=sy_peer(j), device_id_type=MESH)
    load_schur = pltpu.make_async_copy(schur_hbm.at[0, 0], schur, mat_sem.at[1])
    load_inverse = pltpu.make_async_copy(inverse_hbm.at[0, 0], inverse, mat_sem.at[0])
    load_schur.start()
    load_inverse.start()

    nbr = (sx_peer(cols - 1), sx_peer(1), sy_peer(rows - 1), sy_peer(1))
    opposite = (1, 0, 3, 2)
    there = (a > 0, a < cols - 1, b > 0, b < rows - 1)
    mask = [jnp.where(t, 1.0, 0.0).astype(F32) for t in there]
    weight = [jnp.where(t, 0.5, 1.0).astype(F32) for t in there]
    span = [slice(e * edge, (e + 1) * edge) for e in range(4)]
    flat = 1.0 / float(edge) ** 0.5
    ramp_norm = (edge * (edge * edge - 1) / 12.0) ** 0.5
    ramp = (
        lax.broadcasted_iota(jnp.int32, (1, edge), 1).astype(F32) - (edge - 1) / 2.0
    ) * (1.0 / ramp_norm)

    small[0].wait()
    target_row = dest_ref[...]
    target_col = jnp.transpose(
        jnp.broadcast_to(target_row.astype(F32), (128, obs))
    )[:, 0:1].astype(jnp.int32)
    first = lax.broadcasted_iota(jnp.int32, (obs, obs), 0)
    second = lax.broadcasted_iota(jnp.int32, (obs, obs), 1)
    earlier = jnp.where((target_col == target_row) & (first < second), 1.0, 0.0)
    slot_row = jnp.sum(earlier, axis=0, keepdims=True).astype(jnp.int32)
    place = target_row * 4 + slot_row
    small[1].wait()
    small[2].wait()
    node = node_ref[...]
    below = lax.broadcasted_iota(jnp.int32, (128 - realiz, obs), 0)
    tail = jnp.where(
        below == 0,
        (node // 128).astype(F32),
        jnp.where(below == 1, lax.rem(node, 128).astype(F32), 0.0),
    )
    row_data = jnp.concatenate([values_ref[...], tail.astype(BF16)], axis=0)
    for t in range(4):
        part = cols * rows
        spot = lax.broadcasted_iota(jnp.int32, (part, obs), 0) + t * part
        pick = jnp.where(spot == place, 1.0, 0.0).astype(BF16)
        made = lax.dot_general(pick, row_data, NT, preferred_element_type=F32)
        obs_send[t * cols // 4 : (t + 1) * cols // 4] = made.reshape(
            cols // 4, chips, 8, 128
        ).astype(BF16)

    pl.semaphore_wait(barrier, rows - 1 + cols - 1)

    for j in range(1, cols):
        pltpu.make_async_remote_copy(
            obs_send.at[lax.rem(a + j, cols)], obs_mid.at[j],
            obs_sem.at[0], obs_sem.at[1],
            device_id=sx_peer(j), device_id_type=MESH,
        ).start()
    obs_mid[0] = obs_send[a]

    small[3].wait()
    inv_rows = coarse_ref[...]
    index = lax.broadcasted_iota(jnp.int32, (8, count), 1)
    sub_col = index // per_col
    sub_row = lax.rem(index // 8, rows)
    side = lax.rem(index, 8) // 2
    shared = (
        ((side == 0) & (sub_col > 0))
        | ((side == 1) & (sub_col < cols - 1))
        | ((side == 2) & (sub_row > 0))
        | ((side == 3) & (sub_row < rows - 1))
    )
    from_west = pltpu.roll(inv_rows, per_col - 2, axis=1)
    from_east = pltpu.roll(inv_rows, count - (per_col - 2), axis=1)
    from_south = pltpu.roll(inv_rows, 6, axis=1)
    from_north = pltpu.roll(inv_rows, count - 6, axis=1)
    across = jnp.where(
        side == 0,
        from_west,
        jnp.where(side == 1, from_east, jnp.where(side == 2, from_south, from_north)),
    )
    combined = jnp.where(shared, 0.5 * (inv_rows + across), inv_rows)
    k_send[...] = jnp.zeros_like(k_send)
    for t in range(cols):
        k_send[t, :, 0:per_col] = combined[:, t * per_col : (t + 1) * per_col]
    for j in range(1, cols):
        pltpu.make_async_remote_copy(
            k_send.at[lax.rem(a + j, cols)], k_got.at[cols - j],
            k_sem.at[0], k_sem.at[1],
            device_id=sx_peer(j), device_id_type=MESH,
        ).start()
    k_got[0] = k_send[a]

    wait_bytes(obs_mid.at[pl.ds(1, cols - 1)], obs_sem.at[1])
    for j in range(1, rows):
        pltpu.make_async_remote_copy(
            obs_mid.at[:, lax.rem(b + j, rows) // 2], obs_got.at[j],
            obs_sem.at[2], obs_sem.at[3],
            device_id=sy_peer(j), device_id_type=MESH,
        ).start()
    obs_got[0] = obs_mid[:, b // 2]

    wait_bytes(k_got.at[pl.ds(1, cols - 1)], k_sem.at[1])
    k_row[...] = k_got[...].reshape(cols * 8, 128)
    side_copy = [
        pltpu.make_async_remote_copy(
            k_row, k_side.at[i], side_sem.at[0, i], side_sem.at[1, i],
            device_id=sy_peer(step), device_id_type=MESH,
        )
        for i, step in ((0, 1), (1, rows - 1))
    ]
    for copy in side_copy:
        copy.start()

    edge_of = lax.broadcasted_iota(jnp.int32, (8, size), 1) // edge
    offset = lax.rem(lax.broadcasted_iota(jnp.int32, (8, size), 1), edge).astype(F32)
    function = lax.broadcasted_iota(jnp.int32, (8, size), 0)
    basis = jnp.where(
        edge_of == function // 2,
        jnp.where(
            lax.rem(function, 2) == 0, flat, (offset - (edge - 1) / 2.0) * (1.0 / ramp_norm)
        ),
        0.0,
    ).astype(F32)
    basis3 = jnp.concatenate(split(basis, 3), axis=0)
    load_schur.wait()
    for e in range(4):
        made = jnp.dot(basis3, schur[:, span[e]], preferred_element_type=F32)
        sb_ref[:, span[e]] = jnp.concatenate(
            split(made[0:8] + made[8:16] + made[16:24], 2), axis=0
        )
    state[0] = jnp.ones_like(state[0])
    state[1] = jnp.zeros_like(state[1])
    x_ref[...] = jnp.zeros_like(x_ref)
    d_ref[...] = jnp.zeros_like(d_ref)
    s_ref[...] = jnp.zeros_like(s_ref)
    t_ref[...] = jnp.zeros_like(t_ref)
    pay1[...] = jnp.zeros_like(pay1)

    wait_bytes(obs_got.at[pl.ds(1, rows - 1)], obs_sem.at[3])
    got = obs_got[...].astype(F32).reshape(cols * rows * 8, 128)
    own_half = lax.rem(lax.broadcasted_iota(jnp.int32, (cols * rows * 8, 1), 0), 8) // 4
    got_node = got[:, realiz : realiz + 1] * 128.0 + got[:, realiz + 1 : realiz + 2]
    got_node = jnp.where(own_half == lax.rem(b, 2), got_node.astype(jnp.int32), -1)
    got_values = jnp.transpose(got)[0:realiz].astype(BF16)

    def sch_copy(i, parity=0):
        e, part = i % 4, i // 4
        at = opposite[e] + 4 * part * (1 + parity)
        return pltpu.make_async_remote_copy(
            sch_send.at[i], sch_got.at[at], sch_sem.at[0, i], sch_sem.at[1, at],
            device_id=nbr[e], device_id_type=MESH,
        )

    def lin_copy(i, parity=0):
        e, part = i % 4, i // 4
        at = opposite[e] + 4 * part * (1 + parity)
        return pltpu.make_async_remote_copy(
            lin_send.at[i], lin_got.at[at], lin_sem.at[0, i], lin_sem.at[1, at],
            device_id=nbr[e], device_id_type=MESH,
        )

    def send_partial(e, y):
        y_ref[:, span[e]] = y
        high, low = split(y, 2)
        sch_send[e] = high
        sch_copy(e).start()
        sch_send[4 + e] = low

    def send_payload(parity):
        for j in range(1, rows):
            pltpu.make_async_remote_copy(
                pay1, got1.at[parity, b], out_sem.at[0], one_sem.at[parity],
                device_id=sy_peer(j), device_id_type=MESH,
            ).start()
        got1[parity, b] = pay1[...]
        for e in range(4):
            sch_copy(4 + e, parity).start()

    def pass_payload(parity):
        wait_bytes(got1.at[parity, pl.ds(0, rows - 1)], one_sem.at[parity])
        wait_bytes(got1.at[parity, pl.ds(0, rows - 1)], out_sem.at[0])
        gathered = got1[parity]
        high, low = split(gathered.reshape(rows * 8, 128), 2)
        stack = jnp.concatenate([high, low, high], axis=0)
        partial = jnp.dot(k_cat[...], stack, preferred_element_type=F32)
        sums = jnp.sum(gathered, axis=0)
        left = lax.broadcasted_iota(jnp.int32, (8, 128), 1) < realiz
        for j in range(1, cols):
            pay2[j] = jnp.where(left, partial[j * 8 : (j + 1) * 8], sums)
            pltpu.make_async_remote_copy(
                pay2.at[j], got2.at[parity, j], out_sem.at[1], two_sem.at[parity],
                device_id=sx_peer(j), device_id_type=MESH,
            ).start()
        got2[parity, 0] = jnp.where(left, partial[0:8], sums)

    def take_payload(parity):
        wait_bytes(got2.at[parity, pl.ds(1, cols - 1)], two_sem.at[parity])
        wait_bytes(got2.at[parity, pl.ds(1, cols - 1)], out_sem.at[1])
        return jnp.transpose(jnp.sum(got2[parity], axis=0))

    def finish_image(e, parity):
        sch_copy(4 + e, parity).wait_send()
        sch_copy(4 + opposite[e], parity).wait_recv()
        return y_ref[:, span[e]] + mask[e] * sch_got[4 + 4 * parity + e].astype(F32)

    def take_high(e):
        sch_copy(e).wait_send()
        sch_copy(opposite[e]).wait_recv()
        y_ref[:, span[e]] = y_ref[:, span[e]] + mask[e] * sch_got[e].astype(F32)

    def put_y(e):
        high, low = split(weight[e] * y_ref[:, span[e]], 2)
        yb_ref[0:realiz, span[e]] = high
        yb_ref[realiz:, span[e]] = low

    half = 2 * edge

    def begin_product(operand, matrix):
        for e in range(4):
            acc_ref[:, span[e]] = jnp.dot(
                operand[:, half:], matrix[half:, span[e]], preferred_element_type=F32
            )

    def begin_g():
        acc_g[...] = lax.dot_general(
            sb_ref[:, half:], zb_ref[:, half:], NT, preferred_element_type=F32
        )

    def end_product(operand, matrix, e):
        return acc_ref[:, span[e]] + jnp.dot(
            operand[:, :half], matrix[:half, span[e]], preferred_element_type=F32
        )

    def apply_inverse(parity):
        pass_payload(parity)
        for e in (2, 3):
            take_high(e)
            y_ref[:, span[e]] = finish_image(e, parity)
            put_y(e)
        for e in (0, 1):
            take_high(e)
            put_y(e)
        for e in range(4):
            made = jnp.dot(yb_ref[...], inverse[:, span[e]], preferred_element_type=F32)
            local = weight[e] * (made[0:realiz] + made[realiz:])
            high, low = split(local, 2)
            lin_send[e] = high
            lin_copy(e).start()
            lin_send[4 + e] = low
            h_ref[:, span[e]] = local
        for e in range(4):
            lin_copy(4 + e, parity).start()

    def coarse_part(e, total):
        return (
            total[0:realiz, 2 * e : 2 * e + 1] * flat
            + total[0:realiz, 2 * e + 1 : 2 * e + 2] * ramp
        )

    def take_lin(e):
        lin_copy(e).wait_send()
        lin_copy(opposite[e]).wait_recv()
        return mask[e] * lin_got[e].astype(F32)

    def take_low(e, alpha, once, parity):
        lin_copy(4 + opposite[e], parity).wait_recv()
        low = mask[e] * lin_got[4 + 4 * parity + e].astype(F32)
        t_ref[:, span[e]] = t_ref[:, span[e]] + once * low
        late_ref[:, span[e]] = alpha * low

    def put_z(e, z):
        z_ref[:, span[e]] = z
        high, low = split(z, 2)
        zb_ref[0:realiz, span[e]] = high
        zb_ref[realiz:, span[e]] = low

    for e in range(4):
        at = lax.broadcasted_iota(jnp.int32, (cols * rows * 8, edge), 1) + e * edge
        hot = jnp.where(at == got_node, 1.0, 0.0).astype(BF16)
        send_partial(e, jnp.dot(got_values, hot, preferred_element_type=F32))
    loads = jnp.concatenate(split(y_ref[...], 2), axis=0)
    made = lax.dot_general(basis3, loads, NT, preferred_element_type=F32)
    made = made[0:8] + made[8:16] + made[16:24]
    pay1[:, 0:realiz] = made[:, 0:realiz] + made[:, realiz:]
    send_payload(1)

    for copy in side_copy:
        copy.wait_recv()
    rows_here = k_row[...]
    line = lax.broadcasted_iota(jnp.int32, (cols * 8, 1), 0)
    where_to = lax.rem(line // 8 + a, cols)
    line_side = lax.rem(line, 8) // 2
    k_west = jnp.where(where_to > 0, pltpu.roll(rows_here, 6, axis=0), 0.0)
    k_east = jnp.where(
        where_to < cols - 1, pltpu.roll(rows_here, cols * 8 - 6, axis=0), 0.0
    )
    k_south = mask[2] * pltpu.roll(k_side[0], cols * 8 - 2, axis=0)
    k_north = mask[3] * pltpu.roll(k_side[1], 2, axis=0)
    scale = jnp.where(
        line_side == 0,
        jnp.where(where_to > 0, 0.5, 1.0),
        jnp.where(
            line_side == 1,
            jnp.where(where_to < cols - 1, 0.5, 1.0),
            jnp.where(line_side == 2, weight[2], weight[3]),
        ),
    )
    rows_across = jnp.where(
        line_side == 0,
        k_west,
        jnp.where(line_side == 1, k_east, jnp.where(line_side == 2, k_south, k_north)),
    )
    k_high, k_low = split((scale * (rows_here + rows_across))[:, 0:per_col], 2)
    k_cat[...] = jnp.concatenate([k_high, k_high, k_low], axis=1)
    load_inverse.wait()

    apply_inverse(1)
    for e in (0, 1):
        r_ref[:, span[e]] = finish_image(e, 1)
    for e in (2, 3):
        r_ref[:, span[e]] = y_ref[:, span[e]]
    total = take_payload(1)
    for e in (2, 3, 0, 1):
        put_z(e, h_ref[:, span[e]] + coarse_part(e, total) + take_lin(e))
        if e == 3:
            begin_product(zb_ref, schur)
            begin_g()
    state[2] = -jnp.ones_like(state[2])

    def apply_schur(parity):
        sum_rz = jnp.zeros((realiz, 128), F32)
        sum_zy = jnp.zeros((realiz, 128), F32)
        sum_zs = jnp.zeros((realiz, 128), F32)
        for e in range(4):
            made = end_product(zb_ref, schur, e)
            y = made[0:realiz] + made[realiz:]
            send_partial(e, y)
            z = z_ref[:, span[e]]
            zw = weight[e] * z
            zy, zs, rz = z * y, zw * s_ref[:, span[e]], zw * r_ref[:, span[e]]
            for t in range(edge // 128):
                tile = slice(t * 128, (t + 1) * 128)
                sum_rz += rz[:, tile]
                sum_zy += zy[:, tile]
                sum_zs += zs[:, tile]
        made = acc_g[...] + lax.dot_general(
            sb_ref[:, :half], zb_ref[:, :half], NT, preferred_element_type=F32
        )
        made = made[0:8] + made[8:16]
        pay1[:, 0:realiz] = made[:, 0:realiz] + made[:, realiz:]
        lane = lax.broadcasted_iota(jnp.int32, (realiz, 128), 1)
        dots = jnp.where(
            lane == 0,
            jnp.sum(sum_rz, axis=1, keepdims=True),
            jnp.where(
                lane == 1,
                jnp.sum(sum_zy, axis=1, keepdims=True),
                jnp.where(lane == 2, jnp.sum(sum_zs, axis=1, keepdims=True), 0.0),
            ),
        )
        pay1[:, realiz:] = jnp.transpose(dots)[0:8]
        send_payload(parity)

    def factors(total):
        sums = total[realiz : 2 * realiz]
        rz = sums[:, 0:1]
        beta = rz / state[0, :, 0:1]
        curv = sums[:, 1:2] + beta * (2.0 * sums[:, 2:3] + beta * state[1, :, 0:1])
        state[0] = jnp.broadcast_to(rz, (realiz, 128))
        state[1] = jnp.broadcast_to(curv, (realiz, 128))
        state[2] = jnp.broadcast_to(rz / curv, (realiz, 128))
        return rz / curv, beta

    def advance(e, alpha, beta):
        image = y_ref[:, span[e]] + beta * s_ref[:, span[e]]
        s_ref[:, span[e]] = image
        direction = z_ref[:, span[e]] + beta * d_ref[:, span[e]]
        d_ref[:, span[e]] = direction
        x_ref[:, span[e]] = x_ref[:, span[e]] + alpha * direction
        r_ref[:, span[e]] = r_ref[:, span[e]] - alpha * image

    def step(k, carry):
        parity = lax.rem(k, 2)
        apply_schur(parity)
        for e in range(4):
            lin_copy(4 + e, 1 - parity).wait_send()
        apply_inverse(parity)
        for e in range(4):
            take_low(e, state[2, :, 0:1], jnp.where(k > 0, 1.0, 0.0).astype(F32), 1 - parity)
        for e in (0, 1):
            y_ref[:, span[e]] = finish_image(e, parity)
        total = take_payload(parity)
        alpha, beta = factors(total)
        for e in range(4):
            advance(e, alpha, beta)
            z_ref[:, span[e]] = z_ref[:, span[e]] - late_ref[:, span[e]]
            moved = h_ref[:, span[e]] + coarse_part(e, total) + beta * t_ref[:, span[e]]
            t_ref[:, span[e]] = moved
            z_ref[:, span[e]] = z_ref[:, span[e]] - alpha * moved
        for e in (2, 3, 0, 1):
            came = take_lin(e)
            t_ref[:, span[e]] = t_ref[:, span[e]] + came
            put_z(e, z_ref[:, span[e]] - alpha * came)
            if e == 3:
                begin_product(zb_ref, schur)
                begin_g()
        return carry

    lax.fori_loop(0, ITERS - 1, step, 0)
    last = (ITERS - 1) % 2
    apply_schur(last)
    for e in range(4):
        lin_copy(4 + e, 1 - last).wait_send()
        lin_copy(4 + opposite[e], 1 - last).wait_recv()
    pass_payload(last)
    for e in range(4):
        take_high(e)
        y_ref[:, span[e]] = finish_image(e, last)
    alpha, beta = factors(take_payload(last))
    for e in range(4):
        advance(e, alpha, beta)

    wait_bytes(obs_mid.at[pl.ds(1, cols - 1)], obs_sem.at[0])
    wait_bytes(obs_got.at[pl.ds(1, rows - 1)], obs_sem.at[2])
    wait_bytes(k_got.at[pl.ds(1, cols - 1)], k_sem.at[0])
    for copy in side_copy:
        copy.wait_send()


def body(cols, rows, obs_values, obs_dest, obs_node, schur, local_inverse, coarse_inverse):
    size = schur.shape[-1]
    edge = size // 4
    realiz = obs_values.shape[1]
    obs = obs_values.shape[0]
    count = coarse_inverse.shape[1]
    vmem = pl.BlockSpec(memory_space=pltpu.VMEM)
    hbm = pl.BlockSpec(memory_space=pltpu.HBM)
    vector = pltpu.VMEM((realiz, size), F32)
    halved = pltpu.VMEM((2 * realiz, size), BF16)
    out = jax.ShapeDtypeStruct((realiz, size), F32)
    dma = pltpu.SemaphoreType.DMA
    found, residual = pl.pallas_call(
        functools.partial(kernel, cols, rows),
        out_shape=(out, out),
        in_specs=[hbm] * 6,
        out_specs=(vmem, vmem),
        scratch_shapes=[
            pltpu.VMEM((realiz, obs), BF16),
            pltpu.VMEM((1, obs), jnp.int32),
            pltpu.VMEM((1, obs), jnp.int32),
            pltpu.VMEM((8, count), F32),
            pltpu.VMEM((size, size), BF16),
            pltpu.VMEM((size, size), BF16),
            pltpu.VMEM((cols, rows // 2, 8, 128), BF16),
            pltpu.VMEM((cols, rows // 2, 8, 128), BF16),
            pltpu.VMEM((rows, cols, 8, 128), BF16),
            pltpu.VMEM((cols, 8, 128), F32),
            pltpu.VMEM((cols, 8, 128), F32),
            pltpu.VMEM((cols * 8, 128), F32),
            pltpu.VMEM((2, cols * 8, 128), F32),
            pltpu.VMEM((cols * 8, 3 * 8 * rows), BF16),
            halved, halved,
            vector, vector, vector, vector, vector, vector,
            pltpu.VMEM((2 * realiz, size), F32),
            pltpu.VMEM((16, 2 * realiz), F32),
            pltpu.VMEM((16, size), BF16),
            pltpu.VMEM((8, realiz, edge), BF16),
            pltpu.VMEM((12, realiz, edge), BF16),
            pltpu.VMEM((8, realiz, edge), BF16),
            pltpu.VMEM((12, realiz, edge), BF16),
            pltpu.VMEM((8, 128), F32),
            pltpu.VMEM((2, rows, 8, 128), F32),
            pltpu.VMEM((cols, 8, 128), F32),
            pltpu.VMEM((2, cols, 8, 128), F32),
            pltpu.VMEM((3, realiz, 128), F32), vector,
            dma((4,)), dma((2,)), dma((4,)), dma((2,)), dma((2, 2)),
            dma((2, 12)), dma((2, 12)), dma((2,)), dma((2,)), dma((2,)),
        ],
        compiler_params=pltpu.CompilerParams(
            collective_id=0, has_side_effects=True, vmem_limit_bytes=48 << 20
        ),
    )(
        obs_values.T, obs_dest.reshape(1, obs), obs_node.reshape(1, obs),
        schur, local_inverse, coarse_inverse,
    )
    return found[None, None], residual[None, None]


def solution(mesh):
    placed = (
        P(("sx", "sy"), None),
        P(("sx", "sy"), None),
        P(("sx", "sy")),
        P("sx", "sy", None, None),
        P("sx", "sy", None, None),
        P(("sx", "sy"), None),
    )
    return jax.shard_map(
        functools.partial(body, mesh.shape["sx"], mesh.shape["sy"]),
        mesh=mesh,
        in_specs=placed,
        out_specs=(P("sx", "sy", None, None), P("sx", "sy", None, None)),
        check_vma=False,
    )
```

```python
import functools

import jax
import jax.numpy as jnp
from jax import lax
from jax.experimental import pallas as pl
from jax.experimental.pallas import tpu as pltpu
from jax.sharding import PartitionSpec as P

ITERS = 6
MESH = pl.DeviceIdType.MESH
F32 = jnp.float32
BF16 = jnp.bfloat16
NT = (((1,), (1,)), ((), ()))


def split(value, parts):
    found = []
    for _ in range(parts):
        piece = value.astype(BF16)
        found.append(piece)
        value = value - piece.astype(F32)
    return found


def wait_bytes(ref, sem):
    pltpu.make_async_copy(ref, ref, sem).wait()


def kernel(
    cols, rows,
    values_hbm, dest_hbm, node_hbm, schur_hbm, inverse_hbm, coarse_hbm,
    x_ref, r_ref,
    values_ref, dest_ref, node_ref, coarse_ref, schur, inverse,
    obs_send, obs_mid, obs_got, k_send, k_got, k_row, k_side, k_cat,
    zb_ref, yb_ref, d_ref, s_ref, t_ref, z_ref, y_ref, h_ref, acc_ref, acc_g, sb_ref,
    lin_send, lin_got, sch_send, sch_got,
    pay1, got1, pay2, got2, state, late_ref,
    in_sem, mat_sem, obs_sem, k_sem, side_sem, lin_sem, sch_sem, one_sem, two_sem, out_sem,
):
    a = lax.axis_index("sx")
    b = lax.axis_index("sy")
    size = schur.shape[0]
    edge = size // 4
    realiz = values_ref.shape[0]
    obs = values_ref.shape[1]
    count = coarse_ref.shape[1]
    per_col = 8 * rows
    chips = rows // 2

    def sx_peer(j):
        return (lax.rem(a + j, cols), b)

    def sy_peer(j):
        return (a, lax.rem(b + j, rows))

    small = [
        pltpu.make_async_copy(dest_hbm, dest_ref, in_sem.at[0]),
        pltpu.make_async_copy(node_hbm, node_ref, in_sem.at[1]),
        pltpu.make_async_copy(values_hbm, values_ref, in_sem.at[2]),
        pltpu.make_async_copy(coarse_hbm, coarse_ref, in_sem.at[3]),
    ]
    for copy in small:
        copy.start()
    barrier = pltpu.get_barrier_semaphore()
    for j in range(1, cols):
        pl.semaphore_signal(barrier, inc=1, device_id=sx_peer(j), device_id_type=MESH)
    for j in range(1, rows):
        pl.semaphore_signal(barrier, inc=1, device_id=sy_peer(j), device_id_type=MESH)
    load_schur = pltpu.make_async_copy(schur_hbm.at[0, 0], schur, mat_sem.at[1])
    load_inverse = pltpu.make_async_copy(inverse_hbm.at[0, 0], inverse, mat_sem.at[0])
    load_schur.start()
    load_inverse.start()

    nbr = (sx_peer(cols - 1), sx_peer(1), sy_peer(rows - 1), sy_peer(1))
    opposite = (1, 0, 3, 2)
    there = (a > 0, a < cols - 1, b > 0, b < rows - 1)
    mask = [jnp.where(t, 1.0, 0.0).astype(F32) for t in there]
    weight = [jnp.where(t, 0.5, 1.0).astype(F32) for t in there]
    span = [slice(e * edge, (e + 1) * edge) for e in range(4)]
    flat = 1.0 / float(edge) ** 0.5
    ramp_norm = (edge * (edge * edge - 1) / 12.0) ** 0.5
    ramp = (
        lax.broadcasted_iota(jnp.int32, (1, edge), 1).astype(F32) - (edge - 1) / 2.0
    ) * (1.0 / ramp_norm)

    small[0].wait()
    target_row = dest_ref[...]
    target_col = jnp.transpose(
        jnp.broadcast_to(target_row.astype(F32), (128, obs))
    )[:, 0:1].astype(jnp.int32)
    first = lax.broadcasted_iota(jnp.int32, (obs, obs), 0)
    second = lax.broadcasted_iota(jnp.int32, (obs, obs), 1)
    earlier = jnp.where((target_col == target_row) & (first < second), 1.0, 0.0)
    slot_row = jnp.sum(earlier, axis=0, keepdims=True).astype(jnp.int32)
    place = target_row * 4 + slot_row
    small[1].wait()
    small[2].wait()
    node = node_ref[...]
    below = lax.broadcasted_iota(jnp.int32, (128 - realiz, obs), 0)
    tail = jnp.where(
        below == 0,
        (node // 128).astype(F32),
        jnp.where(below == 1, lax.rem(node, 128).astype(F32), 0.0),
    )
    row_data = jnp.concatenate([values_ref[...], tail.astype(BF16)], axis=0)
    for t in range(4):
        part = cols * rows
        spot = lax.broadcasted_iota(jnp.int32, (part, obs), 0) + t * part
        pick = jnp.where(spot == place, 1.0, 0.0).astype(BF16)
        made = lax.dot_general(pick, row_data, NT, preferred_element_type=F32)
        obs_send[t * cols // 4 : (t + 1) * cols // 4] = made.reshape(
            cols // 4, chips, 8, 128
        ).astype(BF16)

    pl.semaphore_wait(barrier, rows - 1 + cols - 1)

    for j in range(1, cols):
        pltpu.make_async_remote_copy(
            obs_send.at[lax.rem(a + j, cols)], obs_mid.at[j],
            obs_sem.at[0], obs_sem.at[1],
            device_id=sx_peer(j), device_id_type=MESH,
        ).start()
    obs_mid[0] = obs_send[a]

    small[3].wait()
    inv_rows = coarse_ref[...]
    index = lax.broadcasted_iota(jnp.int32, (8, count), 1)
    sub_col = index // per_col
    sub_row = lax.rem(index // 8, rows)
    side = lax.rem(index, 8) // 2
    shared = (
        ((side == 0) & (sub_col > 0))
        | ((side == 1) & (sub_col < cols - 1))
        | ((side == 2) & (sub_row > 0))
        | ((side == 3) & (sub_row < rows - 1))
    )
    from_west = pltpu.roll(inv_rows, per_col - 2, axis=1)
    from_east = pltpu.roll(inv_rows, count - (per_col - 2), axis=1)
    from_south = pltpu.roll(inv_rows, 6, axis=1)
    from_north = pltpu.roll(inv_rows, count - 6, axis=1)
    across = jnp.where(
        side == 0,
        from_west,
        jnp.where(side == 1, from_east, jnp.where(side == 2, from_south, from_north)),
    )
    combined = jnp.where(shared, 0.5 * (inv_rows + across), inv_rows)
    k_send[...] = jnp.zeros_like(k_send)
    for t in range(cols):
        k_send[t, :, 0:per_col] = combined[:, t * per_col : (t + 1) * per_col]
    for j in range(1, cols):
        pltpu.make_async_remote_copy(
            k_send.at[lax.rem(a + j, cols)], k_got.at[cols - j],
            k_sem.at[0], k_sem.at[1],
            device_id=sx_peer(j), device_id_type=MESH,
        ).start()
    k_got[0] = k_send[a]

    wait_bytes(obs_mid.at[pl.ds(1, cols - 1)], obs_sem.at[1])
    for j in range(1, rows):
        pltpu.make_async_remote_copy(
            obs_mid.at[:, lax.rem(b + j, rows) // 2], obs_got.at[j],
            obs_sem.at[2], obs_sem.at[3],
            device_id=sy_peer(j), device_id_type=MESH,
        ).start()
    obs_got[0] = obs_mid[:, b // 2]

    wait_bytes(k_got.at[pl.ds(1, cols - 1)], k_sem.at[1])
    k_row[...] = k_got[...].reshape(cols * 8, 128)
    side_copy = [
        pltpu.make_async_remote_copy(
            k_row, k_side.at[i], side_sem.at[0, i], side_sem.at[1, i],
            device_id=sy_peer(step), device_id_type=MESH,
        )
        for i, step in ((0, 1), (1, rows - 1))
    ]
    for copy in side_copy:
        copy.start()

    edge_of = lax.broadcasted_iota(jnp.int32, (8, size), 1) // edge
    offset = lax.rem(lax.broadcasted_iota(jnp.int32, (8, size), 1), edge).astype(F32)
    function = lax.broadcasted_iota(jnp.int32, (8, size), 0)
    basis = jnp.where(
        edge_of == function // 2,
        jnp.where(
            lax.rem(function, 2) == 0, flat, (offset - (edge - 1) / 2.0) * (1.0 / ramp_norm)
        ),
        0.0,
    ).astype(F32)
    basis3 = jnp.concatenate(split(basis, 3), axis=0)
    load_schur.wait()
    for e in range(4):
        made = jnp.dot(basis3, schur[:, span[e]], preferred_element_type=F32)
        sb_ref[:, span[e]] = jnp.concatenate(
            split(made[0:8] + made[8:16] + made[16:24], 2), axis=0
        )
    state[0] = jnp.ones_like(state[0])
    state[1] = jnp.zeros_like(state[1])
    x_ref[...] = jnp.zeros_like(x_ref)
    d_ref[...] = jnp.zeros_like(d_ref)
    s_ref[...] = jnp.zeros_like(s_ref)
    t_ref[...] = jnp.zeros_like(t_ref)
    pay1[...] = jnp.zeros_like(pay1)

    wait_bytes(obs_got.at[pl.ds(1, rows - 1)], obs_sem.at[3])
    got = obs_got[...].astype(F32).reshape(cols * rows * 8, 128)
    own_half = lax.rem(lax.broadcasted_iota(jnp.int32, (cols * rows * 8, 1), 0), 8) // 4
    got_node = got[:, realiz : realiz + 1] * 128.0 + got[:, realiz + 1 : realiz + 2]
    got_node = jnp.where(own_half == lax.rem(b, 2), got_node.astype(jnp.int32), -1)
    got_values = jnp.transpose(got)[0:realiz].astype(BF16)

    def sch_copy(i, parity=0):
        e, part = i % 4, i // 4
        at = opposite[e] + 4 * part * (1 + parity)
        return pltpu.make_async_remote_copy(
            sch_send.at[i], sch_got.at[at], sch_sem.at[0, i], sch_sem.at[1, at],
            device_id=nbr[e], device_id_type=MESH,
        )

    def lin_copy(i, parity=0):
        e, part = i % 4, i // 4
        at = opposite[e] + 4 * part * (1 + parity)
        return pltpu.make_async_remote_copy(
            lin_send.at[i], lin_got.at[at], lin_sem.at[0, i], lin_sem.at[1, at],
            device_id=nbr[e], device_id_type=MESH,
        )

    def send_partial(e, y):
        y_ref[:, span[e]] = y
        high, low = split(y, 2)
        sch_send[e] = high
        sch_copy(e).start()
        sch_send[4 + e] = low

    def send_payload(parity):
        for j in range(1, rows):
            pltpu.make_async_remote_copy(
                pay1, got1.at[parity, b], out_sem.at[0], one_sem.at[parity],
                device_id=sy_peer(j), device_id_type=MESH,
            ).start()
        got1[parity, b] = pay1[...]
        for e in range(4):
            sch_copy(4 + e, parity).start()

    def pass_payload(parity):
        wait_bytes(got1.at[parity, pl.ds(0, rows - 1)], one_sem.at[parity])
        wait_bytes(got1.at[parity, pl.ds(0, rows - 1)], out_sem.at[0])
        gathered = got1[parity]
        high, low = split(gathered.reshape(rows * 8, 128), 2)
        stack = jnp.concatenate([high, low, high], axis=0)
        partial = jnp.dot(k_cat[...], stack, preferred_element_type=F32)
        sums = jnp.sum(gathered, axis=0)
        left = lax.broadcasted_iota(jnp.int32, (8, 128), 1) < realiz
        for j in range(1, cols):
            pay2[j] = jnp.where(left, partial[j * 8 : (j + 1) * 8], sums)
            pltpu.make_async_remote_copy(
                pay2.at[j], got2.at[parity, j], out_sem.at[1], two_sem.at[parity],
                device_id=sx_peer(j), device_id_type=MESH,
            ).start()
        got2[parity, 0] = jnp.where(left, partial[0:8], sums)

    def take_payload(parity):
        wait_bytes(got2.at[parity, pl.ds(1, cols - 1)], two_sem.at[parity])
        wait_bytes(got2.at[parity, pl.ds(1, cols - 1)], out_sem.at[1])
        return jnp.transpose(jnp.sum(got2[parity], axis=0))

    def finish_image(e, parity):
        sch_copy(4 + e, parity).wait_send()
        sch_copy(4 + opposite[e], parity).wait_recv()
        return y_ref[:, span[e]] + mask[e] * sch_got[4 + 4 * parity + e].astype(F32)

    def take_high(e):
        sch_copy(e).wait_send()
        sch_copy(opposite[e]).wait_recv()
        y_ref[:, span[e]] = y_ref[:, span[e]] + mask[e] * sch_got[e].astype(F32)

    def put_y(e):
        high, low = split(weight[e] * y_ref[:, span[e]], 2)
        yb_ref[0:realiz, span[e]] = high
        yb_ref[realiz:, span[e]] = low

    half = 2 * edge

    def begin_product(operand, matrix):
        for e in range(4):
            acc_ref[:, span[e]] = jnp.dot(
                operand[:, half:], matrix[half:, span[e]], preferred_element_type=F32
            )

    def begin_g():
        acc_g[...] = lax.dot_general(
            sb_ref[:, half:], zb_ref[:, half:], NT, preferred_element_type=F32
        )

    def end_product(operand, matrix, e):
        return acc_ref[:, span[e]] + jnp.dot(
            operand[:, :half], matrix[:half, span[e]], preferred_element_type=F32
        )

    def apply_inverse(parity):
        pass_payload(parity)
        for e in (2, 3):
            take_high(e)
            y_ref[:, span[e]] = finish_image(e, parity)
            put_y(e)
        for e in (0, 1):
            take_high(e)
            put_y(e)
        for e in range(4):
            made = jnp.dot(yb_ref[...], inverse[:, span[e]], preferred_element_type=F32)
            local = weight[e] * (made[0:realiz] + made[realiz:])
            high, low = split(local, 2)
            lin_send[e] = high
            lin_copy(e).start()
            lin_send[4 + e] = low
            h_ref[:, span[e]] = local
        for e in range(4):
            lin_copy(4 + e, parity).start()

    def coarse_part(e, total):
        return (
            total[0:realiz, 2 * e : 2 * e + 1] * flat
            + total[0:realiz, 2 * e + 1 : 2 * e + 2] * ramp
        )

    def take_lin(e):
        lin_copy(e).wait_send()
        lin_copy(opposite[e]).wait_recv()
        return mask[e] * lin_got[e].astype(F32)

    def take_low(e, alpha, once, parity):
        lin_copy(4 + opposite[e], parity).wait_recv()
        low = mask[e] * lin_got[4 + 4 * parity + e].astype(F32)
        t_ref[:, span[e]] = t_ref[:, span[e]] + once * low
        late_ref[:, span[e]] = alpha * low

    def put_z(e, z):
        z_ref[:, span[e]] = z
        high, low = split(z, 2)
        zb_ref[0:realiz, span[e]] = high
        zb_ref[realiz:, span[e]] = low

    for e in range(4):
        at = lax.broadcasted_iota(jnp.int32, (cols * rows * 8, edge), 1) + e * edge
        hot = jnp.where(at == got_node, 1.0, 0.0).astype(BF16)
        send_partial(e, jnp.dot(got_values, hot, preferred_element_type=F32))
    loads = jnp.concatenate(split(y_ref[...], 2), axis=0)
    made = lax.dot_general(basis3, loads, NT, preferred_element_type=F32)
    made = made[0:8] + made[8:16] + made[16:24]
    pay1[:, 0:realiz] = made[:, 0:realiz] + made[:, realiz:]
    send_payload(1)

    for copy in side_copy:
        copy.wait_recv()
    rows_here = k_row[...]
    line = lax.broadcasted_iota(jnp.int32, (cols * 8, 1), 0)
    where_to = lax.rem(line // 8 + a, cols)
    line_side = lax.rem(line, 8) // 2
    k_west = jnp.where(where_to > 0, pltpu.roll(rows_here, 6, axis=0), 0.0)
    k_east = jnp.where(
        where_to < cols - 1, pltpu.roll(rows_here, cols * 8 - 6, axis=0), 0.0
    )
    k_south = mask[2] * pltpu.roll(k_side[0], cols * 8 - 2, axis=0)
    k_north = mask[3] * pltpu.roll(k_side[1], 2, axis=0)
    scale = jnp.where(
        line_side == 0,
        jnp.where(where_to > 0, 0.5, 1.0),
        jnp.where(
            line_side == 1,
            jnp.where(where_to < cols - 1, 0.5, 1.0),
            jnp.where(line_side == 2, weight[2], weight[3]),
        ),
    )
    rows_across = jnp.where(
        line_side == 0,
        k_west,
        jnp.where(line_side == 1, k_east, jnp.where(line_side == 2, k_south, k_north)),
    )
    k_high, k_low = split((scale * (rows_here + rows_across))[:, 0:per_col], 2)
    k_cat[...] = jnp.concatenate([k_high, k_high, k_low], axis=1)
    load_inverse.wait()

    apply_inverse(1)
    for e in (0, 1):
        r_ref[:, span[e]] = finish_image(e, 1)
    for e in (2, 3):
        r_ref[:, span[e]] = y_ref[:, span[e]]
    total = take_payload(1)
    for e in (2, 3, 0, 1):
        put_z(e, h_ref[:, span[e]] + coarse_part(e, total) + take_lin(e))
        if e == 3:
            begin_product(zb_ref, schur)
            begin_g()
    state[2] = -jnp.ones_like(state[2])

    def apply_schur(parity):
        sum_rz = jnp.zeros((realiz, 128), F32)
        sum_zy = jnp.zeros((realiz, 128), F32)
        sum_zs = jnp.zeros((realiz, 128), F32)
        for e in range(4):
            made = end_product(zb_ref, schur, e)
            y = made[0:realiz] + made[realiz:]
            send_partial(e, y)
            z = z_ref[:, span[e]]
            zw = weight[e] * z
            zy, zs, rz = z * y, zw * s_ref[:, span[e]], zw * r_ref[:, span[e]]
            for t in range(edge // 128):
                tile = slice(t * 128, (t + 1) * 128)
                sum_rz += rz[:, tile]
                sum_zy += zy[:, tile]
                sum_zs += zs[:, tile]
        made = acc_g[...] + lax.dot_general(
            sb_ref[:, :half], zb_ref[:, :half], NT, preferred_element_type=F32
        )
        made = made[0:8] + made[8:16]
        pay1[:, 0:realiz] = made[:, 0:realiz] + made[:, realiz:]
        lane = lax.broadcasted_iota(jnp.int32, (realiz, 128), 1)
        dots = jnp.where(
            lane == 0,
            jnp.sum(sum_rz, axis=1, keepdims=True),
            jnp.where(
                lane == 1,
                jnp.sum(sum_zy, axis=1, keepdims=True),
                jnp.where(lane == 2, jnp.sum(sum_zs, axis=1, keepdims=True), 0.0),
            ),
        )
        pay1[:, realiz:] = jnp.transpose(dots)[0:8]
        send_payload(parity)

    def factors(total):
        sums = total[realiz : 2 * realiz]
        rz = sums[:, 0:1]
        beta = rz / state[0, :, 0:1]
        curv = sums[:, 1:2] + beta * (2.0 * sums[:, 2:3] + beta * state[1, :, 0:1])
        state[0] = jnp.broadcast_to(rz, (realiz, 128))
        state[1] = jnp.broadcast_to(curv, (realiz, 128))
        state[2] = jnp.broadcast_to(rz / curv, (realiz, 128))
        return rz / curv, beta

    def advance(e, alpha, beta):
        image = y_ref[:, span[e]] + beta * s_ref[:, span[e]]
        s_ref[:, span[e]] = image
        direction = z_ref[:, span[e]] + beta * d_ref[:, span[e]]
        d_ref[:, span[e]] = direction
        x_ref[:, span[e]] = x_ref[:, span[e]] + alpha * direction
        r_ref[:, span[e]] = r_ref[:, span[e]] - alpha * image

    def step(k, carry):
        parity = lax.rem(k, 2)
        apply_schur(parity)
        for e in range(4):
            lin_copy(4 + e, 1 - parity).wait_send()
        apply_inverse(parity)
        for e in range(4):
            take_low(e, state[2, :, 0:1], jnp.where(k > 0, 1.0, 0.0).astype(F32), 1 - parity)
        for e in (0, 1):
            y_ref[:, span[e]] = finish_image(e, parity)
        total = take_payload(parity)
        alpha, beta = factors(total)
        for e in range(4):
            advance(e, alpha, beta)
            z_ref[:, span[e]] = z_ref[:, span[e]] - late_ref[:, span[e]]
            moved = h_ref[:, span[e]] + coarse_part(e, total) + beta * t_ref[:, span[e]]
            t_ref[:, span[e]] = moved
            z_ref[:, span[e]] = z_ref[:, span[e]] - alpha * moved
        for e in (2, 3, 0, 1):
            came = take_lin(e)
            t_ref[:, span[e]] = t_ref[:, span[e]] + came
            put_z(e, z_ref[:, span[e]] - alpha * came)
            if e == 3:
                begin_product(zb_ref, schur)
                begin_g()
        return carry

    lax.fori_loop(0, ITERS - 1, step, 0)
    last = (ITERS - 1) % 2
    apply_schur(last)
    for e in range(4):
        lin_copy(4 + e, 1 - last).wait_send()
        lin_copy(4 + opposite[e], 1 - last).wait_recv()
    pass_payload(last)
    for e in range(4):
        take_high(e)
        y_ref[:, span[e]] = finish_image(e, last)
    alpha, beta = factors(take_payload(last))
    for e in range(4):
        advance(e, alpha, beta)

    wait_bytes(obs_mid.at[pl.ds(1, cols - 1)], obs_sem.at[0])
    wait_bytes(obs_got.at[pl.ds(1, rows - 1)], obs_sem.at[2])
    wait_bytes(k_got.at[pl.ds(1, cols - 1)], k_sem.at[0])
    for copy in side_copy:
        copy.wait_send()


def body(cols, rows, obs_values, obs_dest, obs_node, schur, local_inverse, coarse_inverse):
    size = schur.shape[-1]
    edge = size // 4
    realiz = obs_values.shape[1]
    obs = obs_values.shape[0]
    count = coarse_inverse.shape[1]
    vmem = pl.BlockSpec(memory_space=pltpu.VMEM)
    hbm = pl.BlockSpec(memory_space=pltpu.HBM)
    vector = pltpu.VMEM((realiz, size), F32)
    halved = pltpu.VMEM((2 * realiz, size), BF16)
    out = jax.ShapeDtypeStruct((realiz, size), F32)
    dma = pltpu.SemaphoreType.DMA
    found, residual = pl.pallas_call(
        functools.partial(kernel, cols, rows),
        out_shape=(out, out),
        in_specs=[hbm] * 6,
        out_specs=(vmem, vmem),
        scratch_shapes=[
            pltpu.VMEM((realiz, obs), BF16),
            pltpu.VMEM((1, obs), jnp.int32),
            pltpu.VMEM((1, obs), jnp.int32),
            pltpu.VMEM((8, count), F32),
            pltpu.VMEM((size, size), BF16),
            pltpu.VMEM((size, size), BF16),
            pltpu.VMEM((cols, rows // 2, 8, 128), BF16),
            pltpu.VMEM((cols, rows // 2, 8, 128), BF16),
            pltpu.VMEM((rows, cols, 8, 128), BF16),
            pltpu.VMEM((cols, 8, 128), F32),
            pltpu.VMEM((cols, 8, 128), F32),
            pltpu.VMEM((cols * 8, 128), F32),
            pltpu.VMEM((2, cols * 8, 128), F32),
            pltpu.VMEM((cols * 8, 3 * 8 * rows), BF16),
            halved, halved,
            vector, vector, vector, vector, vector, vector,
            pltpu.VMEM((2 * realiz, size), F32),
            pltpu.VMEM((16, 2 * realiz), F32),
            pltpu.VMEM((16, size), BF16),
            pltpu.VMEM((8, realiz, edge), BF16),
            pltpu.VMEM((12, realiz, edge), BF16),
            pltpu.VMEM((8, realiz, edge), BF16),
            pltpu.VMEM((12, realiz, edge), BF16),
            pltpu.VMEM((8, 128), F32),
            pltpu.VMEM((2, rows, 8, 128), F32),
            pltpu.VMEM((cols, 8, 128), F32),
            pltpu.VMEM((2, cols, 8, 128), F32),
            pltpu.VMEM((3, realiz, 128), F32), vector,
            dma((4,)), dma((2,)), dma((4,)), dma((2,)), dma((2, 2)),
            dma((2, 12)), dma((2, 12)), dma((2,)), dma((2,)), dma((2,)),
        ],
        compiler_params=pltpu.CompilerParams(
            collective_id=0, has_side_effects=True, vmem_limit_bytes=60 << 20
        ),
    )(
        obs_values.T, obs_dest.reshape(1, obs), obs_node.reshape(1, obs),
        schur, local_inverse, coarse_inverse,
    )
    return found[None, None], residual[None, None]


def solution(mesh):
    placed = (
        P(("sx", "sy"), None),
        P(("sx", "sy"), None),
        P(("sx", "sy")),
        P("sx", "sy", None, None),
        P("sx", "sy", None, None),
        P(("sx", "sy"), None),
    )
    return jax.shard_map(
        functools.partial(body, mesh.shape["sx"], mesh.shape["sy"]),
        mesh=mesh,
        in_specs=placed,
        out_specs=(P("sx", "sy", None, None), P("sx", "sy", None, None)),
        check_vma=False,
    )
```
